32 devices in a mesh: tile: 16 (over z, y, core), freq: 2 (over x).
Axes of the slice: x: 2, y: 2, z: 4, core: 2. Of those that a mesh axis runs over, the one named last changes fastest.
Arguments:
- wavefield: bfloat16 [8, 2, 16384, 256], P('freq', None, 'tile'), may hold values from -6 to 6
- row_factors: bfloat16 [8, 2, 32768, 1024], P('freq', None, 'tile'), may hold values from -0.125 to 0.125
- col_factors: bfloat16 [8, 2, 16384, 2048], P('freq', None, 'tile'), may hold values from -0.1875 to 0.1875
- window_index: int32 [256], replicated, may hold values from 1 to 15
Outputs:
- adjoint_field: float32 [8, 2, 16384, 256], P('freq', None, 'tile')
The draws below stay inside these ranges and needn't reach their ends.
All inputs are finite; a program needn't handle non-finite values.
Results may differ from the reference program's by a relative error of at most 0.0038.
Values may be sent and summed in bfloat16 or wider, within the bound.
No kernel may reach another device: no remote copies, remote signals or barrier semaphores. Data moves between devices by JAX's collectives and lax.ppermute only.
A program may use at most 256 MiB of HBM per device.

```python
import math
import jax
import jax.numpy as jnp
from jax import lax

FREQS = 8
NR = 32768
NS = 16384
TS = 512
RANK = 32
VP = 256
NT = 16
RTILES = 64
CTILES = 32


def set_ends(values, stream_key, low, top_value):
    shape = values.shape
    spot = [jax.random.randint(jax.random.fold_in(stream_key, axis), (), 0, shape[axis]) for axis in range(len(shape))]
    values = values.at[tuple(spot)].set(low)
    longest = shape.index(max(shape))
    spot[longest] = (spot[longest] + 1) % shape[longest]
    return values.at[tuple(spot)].set(top_value)


def level_of(key, shape, shards, low, top_value):
    gain = 1.0
    for dim, parts in shards:
        steps = jax.random.uniform(jax.random.fold_in(jax.random.fold_in(key, 6), dim), (parts,), jnp.float32, low / len(shards), top_value / len(shards))
        gain = gain * jnp.repeat(jnp.exp(steps), shape[dim] // parts).reshape((-1,) + (1,) * (len(shape) - 1 - dim))
    return gain


def centred(stream_key, dims, deviation, most, pieces=(), held_as=jnp.bfloat16):
    entries = jax.random.normal(stream_key, dims, jnp.float32) * deviation
    if len(pieces) > 0:
        entries = level_of(stream_key, dims, pieces, -0.22, 0.18) * entries
    return jnp.clip(entries, min=-most, max=most).astype(held_as)


def setup_inputs(seed: int = 0) -> dict:
    key_of = jax.random.split(jax.random.key(seed), 5)
    wavefield = centred(key_of[0], (FREQS, 2, NS, VP), 1.0, 6.0, ((0, 2), (2, 16)))
    row_factors = centred(key_of[1], (FREQS, 2, NR, CTILES * RANK), (2 * CTILES * RANK) ** -0.5, 0.125, ((0, 2), (2, 16)))
    col_factors = centred(key_of[2], (FREQS, 2, NS, RTILES * RANK), (2 * TS) ** -0.5, 0.1875, ((0, 2), (2, 16)))
    window_index = set_ends(jax.random.randint(key_of[3], (VP,), 1, NT), jax.random.fold_in(key_of[3], 1), 1, NT - 1).astype(jnp.int32)
    return {"wavefield": wavefield, "row_factors": row_factors, "col_factors": col_factors, "window_index": window_index}


def angles(freq_ids):
    times = lax.broadcasted_iota(jnp.int32, (NT, freq_ids.shape[0]), 0)
    return (math.pi / NT) * ((2 * freq_ids[None, :] + 1) * times).astype(jnp.float32)


def forward_one(packed):
    wave, row_f, col_f = packed
    col_view = col_f.astype(jnp.float32).reshape(2, CTILES, TS, RTILES * RANK)
    wave_view = wave.astype(jnp.float32).reshape(2, CTILES, TS, VP)

    def project(left, right):
        return jnp.einsum("csa,csv->cav", left, right)

    real_part = project(col_view[0], wave_view[0]) + project(col_view[1], wave_view[1])
    imag_part = project(col_view[0], wave_view[1]) - project(col_view[1], wave_view[0])
    coeffs = jnp.stack([real_part, imag_part]).astype(jnp.bfloat16).reshape(2, CTILES, RTILES, RANK, VP)
    coeffs = jnp.transpose(coeffs, (0, 2, 1, 3, 4)).reshape(2, RTILES, CTILES * RANK, VP).astype(jnp.float32)
    row_view = row_f.astype(jnp.float32).reshape(2, RTILES, TS, CTILES * RANK)

    def expand(left, right):
        return jnp.einsum("isa,iav->isv", left, right)

    real_out = expand(row_view[0], coeffs[0]) - expand(row_view[1], coeffs[1])
    imag_out = expand(row_view[0], coeffs[1]) + expand(row_view[1], coeffs[0])
    return jnp.stack([real_out, imag_out]).astype(jnp.bfloat16).reshape(2, NR, VP)


def adjoint_one(packed):
    filtered, row_f, col_f = packed
    row_view = row_f.astype(jnp.float32).reshape(2, RTILES, TS, CTILES * RANK)
    filt_view = filtered.astype(jnp.float32).reshape(2, RTILES, TS, VP)

    def contract(left, right):
        return jnp.einsum("isa,isv->iav", left, right)

    real_part = contract(row_view[0], filt_view[0]) + contract(row_view[1], filt_view[1])
    imag_part = contract(row_view[0], filt_view[1]) - contract(row_view[1], filt_view[0])
    returned = jnp.stack([real_part, imag_part]).astype(jnp.bfloat16).reshape(2, RTILES, CTILES, RANK, VP)
    returned = jnp.transpose(returned, (0, 2, 1, 3, 4)).reshape(2, CTILES, RTILES * RANK, VP).astype(jnp.float32)
    col_view = col_f.astype(jnp.float32).reshape(2, CTILES, TS, RTILES * RANK)

    def spread(left, right):
        return jnp.einsum("csa,cav->csv", left, right)

    real_out = spread(col_view[0], returned[0]) - spread(col_view[1], returned[1])
    imag_out = spread(col_view[0], returned[1]) + spread(col_view[1], returned[0])
    return jnp.stack([real_out, imag_out]).reshape(2, NS, VP)


def reference(wavefield, row_factors, col_factors, window_index):
    spectra = lax.map(forward_one, (wavefield, row_factors, col_factors))
    freq_ids = lax.iota(jnp.int32, FREQS)
    phases = angles(freq_ids)
    cosine = 0.25 * jnp.cos(phases)
    sine = 0.25 * jnp.sin(phases)
    high = lax.Precision.HIGHEST
    timed = jnp.einsum("tk,krv->trv", cosine, spectra[:, 0].astype(jnp.float32), precision=high)
    timed = timed - jnp.einsum("tk,krv->trv", sine, spectra[:, 1].astype(jnp.float32), precision=high)
    time_mask = (lax.broadcasted_iota(jnp.int32, (NT, VP), 0) < window_index[None, :]).astype(jnp.float32)
    windowed = timed * time_mask[:, None, :]
    real_part = jnp.einsum("tk,trv->krv", cosine, windowed, precision=high)
    imag_part = -jnp.einsum("tk,trv->krv", sine, windowed, precision=high)
    filtered = jnp.stack([real_part, imag_part], 1).astype(jnp.bfloat16)
    return lax.map(adjoint_one, (filtered, row_factors, col_factors))
```

```python
import functools
import math

import jax
import jax.numpy as jnp
from jax import lax
from jax.experimental import pallas as pl
from jax.experimental.pallas import tpu as pltpu
from jax.sharding import PartitionSpec as P

TS = 512
RANK = 32
NT = 16
CHUNKS = 2
GROUP = 4
VMEM_BYTES = 67043328


def angles(freq_ids):
    times = lax.broadcasted_iota(jnp.int32, (NT, freq_ids.shape[0]), 0)
    return math.pi / NT * ((2 * freq_ids[None, :] + 1) * times).astype(jnp.float32)


def call(kernel, name, grid, prefetch, in_specs, out_specs, out_shape, scratch, flops, nbytes, after, **kw):
    count = prefetch + len(in_specs)
    inner = kernel
    if after is not None:
        in_specs = in_specs + [pl.BlockSpec(memory_space=pl.ANY)]

        def inner(*refs):
            kernel(*refs[:count], *refs[count + 1 :])

    made = pl.pallas_call(
        inner,
        name=name,
        grid_spec=pltpu.PrefetchScalarGridSpec(
            num_scalar_prefetch=prefetch,
            grid=grid,
            in_specs=in_specs,
            out_specs=out_specs,
            scratch_shapes=scratch,
        ),
        out_shape=out_shape,
        cost_estimate=pl.CostEstimate(flops=flops, bytes_accessed=nbytes, transcendentals=0),
        compiler_params=pltpu.CompilerParams(vmem_limit_bytes=VMEM_BYTES),
        **kw,
    )
    return made if after is None else lambda *args: made(*args, after)


def dot(left, right):
    return jnp.dot(left, right, preferred_element_type=jnp.float32)


def turned(left, right):
    return lax.dot_general(left, right, (((0,), (0,)), ((), ())), preferred_element_type=jnp.float32)


def project_kernel(dims, v_ref, w_ref, out, wave):
    col_local, row_local, width = dims
    span = row_local * RANK

    @pl.when(pl.program_id(1) == 0)
    def _():
        wave[:width] = w_ref[0, 0].T
        wave[width:] = w_ref[0, 1].T

    for c in range(col_local):
        rows = slice(c * TS, (c + 1) * TS)
        with_real = dot(wave[:, rows], v_ref[0, 0, rows])
        with_imag = dot(wave[:, rows], v_ref[0, 1, rows])
        real = with_real[:width] + with_imag[width:]
        imag = with_real[width:] - with_imag[:width]
        both = jnp.concatenate([real, imag], 0).astype(jnp.bfloat16).T
        for d in range(GROUP):
            for i in range(row_local):
                start = d * span + i * RANK
                out[d, 0, i, c * RANK : (c + 1) * RANK] = both[start : start + RANK]


def project(col_factors, wavefield, piece, chunk, width, tiles, after):
    first, freqs = piece
    _, _, src_rows, cols = col_factors.shape
    col_local = src_rows // TS
    row_local = cols // RANK // tiles
    lanes = GROUP * row_local * RANK
    shape = (tiles, freqs, row_local, col_local * RANK, 2 * width)
    return call(
        functools.partial(project_kernel, (col_local, row_local, width)),
        "project",
        (freqs, tiles // GROUP),
        0,
        [
            pl.BlockSpec((1, 2, src_rows, lanes), lambda f, g: (first + f, 0, 0, g)),
            pl.BlockSpec((1, 2, src_rows, width), lambda f, g: (first + f, 0, 0, chunk)),
        ],
        pl.BlockSpec((GROUP, 1) + shape[2:], lambda f, g: (g, f, 0, 0, 0)),
        jax.ShapeDtypeStruct(shape, jnp.bfloat16),
        [pltpu.VMEM((2 * width, src_rows), jnp.bfloat16)],
        8 * freqs * src_rows * cols * width,
        freqs * 4 * src_rows * (cols + 2 * width),
        after,
    )(col_factors, wavefield)


def expand_kernel(dims, pos, u_ref, got, *refs):
    shares, width = dims
    outs, stage = refs[:shares], refs[shares]
    coeffs = got[:, 0, 0].reshape(-1, 2 * width)
    with_real = dot(u_ref[0, 0], coeffs)
    with_imag = dot(u_ref[0, 1], coeffs)
    stage[:, :width] = (with_real[:, :width] - with_imag[:, width:]).astype(jnp.bfloat16)
    stage[:, width:] = (with_real[:, width:] + with_imag[:, :width]).astype(jnp.bfloat16)
    share = TS // shares
    for g in range(shares):
        rows = pl.ds(pl.multiple_of((pos[0] ^ g) * share, share), share)
        outs[g][0, 0] = stage[rows]


def expand(pos, row_factors, piece, got, shares, after):
    first, freqs = piece
    _, _, rec_rows, cols = row_factors.shape
    row_local = rec_rows // TS
    tiles, _, _, step, both = got.shape
    shape = (freqs, row_local, TS // shares, both)
    return call(
        functools.partial(expand_kernel, (shares, both // 2)),
        "expand",
        (freqs, row_local),
        1,
        [
            pl.BlockSpec((1, 2, TS, cols), lambda f, i, s: (first + f, 0, i, 0)),
            pl.BlockSpec((tiles, 1, 1, step, both), lambda f, i, s: (0, f, i, 0, 0)),
        ],
        [pl.BlockSpec((1, 1, TS // shares, both), lambda f, i, s: (f, i, 0, 0))] * shares,
        [jax.ShapeDtypeStruct(shape, jnp.bfloat16)] * shares,
        [pltpu.VMEM((TS, both), jnp.bfloat16)],
        4 * freqs * rec_rows * cols * both,
        freqs * 2 * (rec_rows * (2 * cols + both) + row_local * cols * both),
        after,
    )(pos, row_factors, got)


def window_kernel(dims, cosine, sine, index_ref, *refs):
    shares, took, gave, rows, slab, width = dims
    ins, outs = refs[: shares * len(took)], refs[shares * len(took) :]
    half = NT // 2
    masks = [t < index_ref[...] for t in range(NT)]

    def planes(arrays, pieces):
        return [
            (arrays[p * shares + g], f)
            for g in range(shares)
            for p, (_, freqs) in enumerate(pieces)
            for f in range(freqs)
        ]

    def body(n, carry):
        at = pl.ds(pl.multiple_of(n * slab, slab), slab)
        real = [ref[f, 0, at, :width].astype(jnp.float32) for ref, f in planes(ins, took)]
        imag = [ref[f, 0, at, width:].astype(jnp.float32) for ref, f in planes(ins, took)]
        count = len(real)
        even = [sum(cosine[t, k] * real[k] for k in range(count)) for t in range(half)]
        odd = [None] + [sum(sine[t, k] * imag[k] for k in range(count)) for t in range(1, half + 1)]
        zero = jnp.zeros_like(real[0])

        def keep(t, value):
            return jnp.where(masks[t], value, zero)

        diff = [keep(0, even[0])]
        total = [None]
        for t in range(1, half):
            one = keep(t, even[t] - odd[t])
            other = keep(NT - t, -even[t] - odd[t])
            diff.append(one - other)
            total.append(one + other)
        total.append(keep(half, -odd[half]))
        for k, (ref, f) in enumerate(planes(outs, gave)):
            out = sum(cosine[t, k] * diff[t] for t in range(half))
            ref[f, 0, at, :width] = out.astype(jnp.bfloat16)
            out = -sum(sine[t, k] * total[t] for t in range(1, half + 1))
            ref[f, 0, at, width:] = out.astype(jnp.bfloat16)
        return carry

    lax.fori_loop(0, rows // slab, body, 0)


def window(cosine, sine, index, parts, took, gave, chunk):
    shares = len(parts[0])
    _, row_local, rows, both = parts[0][0].shape

    def spec(freqs):
        return pl.BlockSpec((freqs, 1, rows, both), lambda i, c, s: (0, i, 0, 0))

    size = sum(part.size for group in parts for part in group)
    made = call(
        functools.partial(window_kernel, (shares, took, gave, rows, 16, both // 2)),
        "window",
        (row_local,),
        2,
        [pl.BlockSpec((1, both // 2), lambda i, c, s: (0, chunk))]
        + [spec(freqs) for _, freqs in took for _ in range(shares)],
        [spec(freqs) for _, freqs in gave for _ in range(shares)],
        [
            jax.ShapeDtypeStruct((freqs, row_local, rows, both), jnp.bfloat16)
            for _, freqs in gave
            for _ in range(shares)
        ],
        [],
        2 * NT * size,
        4 * size,
        None,
    )(cosine, sine, index, *[part for group in parts for part in group])
    return [made[p * shares : (p + 1) * shares] for p in range(len(gave))]


def contract_kernel(dims, pos, u_ref, *refs):
    tiles, shares, col_local, width = dims
    ins, out, stage = refs[:shares], refs[shares], refs[shares + 1]
    share = TS // shares
    for g in range(shares):
        stage[pl.ds(pl.multiple_of((pos[0] ^ g) * share, share), share)] = ins[g][0, 0]
    with_real = turned(stage[...], u_ref[0, 0])
    with_imag = turned(stage[...], u_ref[0, 1])
    real = with_real[:width] + with_imag[width:]
    imag = with_real[width:] - with_imag[:width]
    both = jnp.concatenate([real, imag], 0).astype(jnp.bfloat16).T
    out[:, 0] = both.reshape(tiles, col_local, RANK, 2 * width)


def contract(pos, row_factors, piece, parts, tiles, after):
    first, freqs = piece
    _, _, rec_rows, cols = row_factors.shape
    row_local = rec_rows // TS
    shares = len(parts)
    share, both = parts[0].shape[2:]
    col_local = cols // RANK // tiles
    shape = (tiles, freqs, col_local, row_local * RANK, both)
    return call(
        functools.partial(contract_kernel, (tiles, shares, col_local, both // 2)),
        "contract",
        (freqs, row_local),
        1,
        [pl.BlockSpec((1, 2, TS, cols), lambda f, i, s: (first + f, 0, i, 0))]
        + [pl.BlockSpec((1, 1, share, both), lambda f, i, s: (f, i, 0, 0))] * shares,
        pl.BlockSpec((tiles, 1, col_local, RANK, both), lambda f, i, s: (0, f, 0, i, 0)),
        jax.ShapeDtypeStruct(shape, jnp.bfloat16),
        [pltpu.VMEM((TS, both), jnp.bfloat16)],
        4 * freqs * rec_rows * cols * both,
        freqs * 2 * (rec_rows * (2 * cols + both) + row_local * cols * both),
        after,
    )(pos, row_factors, *parts)


def spread_kernel(dims, v_ref, got, *refs):
    width = dims
    out = refs[-1]
    coeffs = got[:, 0, 0].reshape(-1, 2 * width)
    with_real = dot(v_ref[0, 0], coeffs)
    with_imag = dot(v_ref[0, 1], coeffs)
    out[0, 0] = with_real[:, :width] - with_imag[:, width:]
    out[0, 1] = with_real[:, width:] + with_imag[:, :width]


def spread(col_factors, piece, got, chunk, points, before, after):
    first, freqs = piece
    total, _, src_rows, cols = col_factors.shape
    tiles, _, _, step, both = got.shape
    carried = 0 if before is None else 1
    return call(
        functools.partial(spread_kernel, both // 2),
        "spread",
        (freqs, src_rows // TS),
        0,
        [
            pl.BlockSpec((1, 2, TS, cols), lambda f, c: (first + f, 0, c, 0)),
            pl.BlockSpec((tiles, 1, 1, step, both), lambda f, c: (0, f, c, 0, 0)),
        ]
        + [pl.BlockSpec(memory_space=pl.ANY)] * carried,
        pl.BlockSpec((1, 2, TS, both // 2), lambda f, c: (first + f, 0, c, chunk)),
        jax.ShapeDtypeStruct((total, 2, src_rows, points), jnp.float32),
        [],
        4 * freqs * src_rows * cols * both,
        freqs * 4 * (src_rows * (cols + both) + cols * both),
        after,
        input_output_aliases={2: 0} if carried else {},
    )(col_factors, got, *([before] if carried else []))


def send(array, axis, size, mask):
    if mask == 0:
        return array
    return lax.ppermute(array, axis, [(n, n ^ mask) for n in range(size)])


def trade(array):
    return lax.all_to_all(array, "tile", 0, 0, tiled=True)


def local(tiles, shares, wavefield, row_factors, col_factors, window_index):
    freqs = wavefield.shape[0]
    points = wavefield.shape[3]
    width = points // CHUNKS
    share = lax.axis_index("freq")
    pos = share.reshape(1).astype(jnp.int32)
    owners = share ^ lax.iota(jnp.int32, shares)
    ids = (owners[:, None] * freqs + lax.iota(jnp.int32, freqs)[None, :]).reshape(-1)
    phases = angles(ids)
    cosine = 0.25 * jnp.cos(phases)
    sine = 0.25 * jnp.sin(phases)
    index = window_index.reshape(1, points)

    whole = ((0, freqs),)
    took = [whole] * CHUNKS
    gave = [whole] * CHUNKS
    if freqs > 1:
        took[0] = ((0, 1), (1, freqs - 1))
        gave[-1] = ((0, freqs - 1), (freqs - 1, 1))

    sent = []
    token = None
    for h in range(CHUNKS):
        sent.append([])
        for piece in took[h]:
            token = project(col_factors, wavefield, piece, h, width, tiles, token)
            sent[h].append(trade(token))
    back = []
    for h in range(CHUNKS):
        parts = []
        for piece, got in zip(took[h], sent[h]):
            made = expand(pos, row_factors, piece, got, shares, token)
            token = made[0]
            parts.append([send(part, "freq", shares, m) for m, part in enumerate(made)])
        parts = window(cosine, sine, index, parts, took[h], gave[h], h)
        parts = [[send(part, "freq", shares, m) for m, part in enumerate(group)] for group in parts]
        back.append([])
        token = None
        for piece, group in zip(gave[h], parts):
            token = contract(pos, row_factors, piece, group, tiles, token)
            back[h].append(trade(token))
    result = None
    for h in range(CHUNKS):
        for piece, got in zip(gave[h], back[h]):
            result = spread(col_factors, piece, got, h, points, result, token)
            token = None
    return result


def solution(mesh):
    spec = P("freq", None, "tile", None)
    body = functools.partial(local, mesh.shape["tile"], mesh.shape["freq"])
    return jax.shard_map(
        body, mesh=mesh, in_specs=(spec, spec, spec, P()), out_specs=spec, check_vma=False
    )
```

```python
import functools
import math

import jax
import jax.numpy as jnp
from jax import lax
from jax.experimental import pallas as pl
from jax.experimental.pallas import tpu as pltpu
from jax.sharding import PartitionSpec as P


TS = 512
RANK = 32
NT = 16
CHUNKS = 2
GROUP = 4
VMEM_BYTES = 67043328


def angles(freq_ids):
    times = lax.broadcasted_iota(jnp.int32, (NT, freq_ids.shape[0]), 0)
    return math.pi / NT * ((2 * freq_ids[None, :] + 1) * times).astype(jnp.float32)


def call(kernel, grid, prefetch, in_specs, out_specs, out_shape, scratch, flops, nbytes, after, **kw):
    count = prefetch + len(in_specs)
    inner = kernel
    if after is not None:
        in_specs = in_specs + [pl.BlockSpec(memory_space=pl.ANY)]

        def inner(*refs):
            kernel(*refs[:count], *refs[count + 1 :])

    made = pl.pallas_call(
        inner,
        grid_spec=pltpu.PrefetchScalarGridSpec(
            num_scalar_prefetch=prefetch,
            grid=grid,
            in_specs=in_specs,
            out_specs=out_specs,
            scratch_shapes=scratch,
        ),
        out_shape=out_shape,
        cost_estimate=pl.CostEstimate(flops=flops, bytes_accessed=nbytes, transcendentals=0),
        compiler_params=pltpu.CompilerParams(vmem_limit_bytes=VMEM_BYTES),
        **kw,
    )
    return made if after is None else lambda *args: made(*args, after)


def dot(left, right):
    return jnp.dot(left, right, preferred_element_type=jnp.float32)


def turned(left, right):
    return lax.dot_general(left, right, (((0,), (0,)), ((), ())), preferred_element_type=jnp.float32)


def project_kernel(dims, pos, v_ref, w_ref, *refs):
    groups, col_local, row_local, width, split = dims
    span = row_local * RANK
    outs = refs[: groups * GROUP if split else 1]
    wave = refs[len(outs)]

    @pl.when(pl.program_id(1) == 0)
    def _():
        wave[:width] = w_ref[0, 0].T
        wave[width:] = w_ref[0, 1].T

    for c in range(col_local):
        rows = slice(c * TS, (c + 1) * TS)
        to = slice(c * RANK, (c + 1) * RANK)
        with_real = dot(wave[:, rows], v_ref[0, 0, rows])
        with_imag = dot(wave[:, rows], v_ref[0, 1, rows])
        real = with_real[:width] + with_imag[width:]
        imag = with_real[width:] - with_imag[:width]
        both = jnp.concatenate([real, imag], 0).astype(jnp.bfloat16).T
        if not split:
            for d in range(GROUP):
                for i in range(row_local):
                    start = d * span + i * RANK
                    outs[0][d, 0, i, to] = both[start : start + RANK]
            continue
        stage = refs[-1]
        stage[...] = both
        for high in range(groups):

            @pl.when(pl.program_id(1) == high)
            def _():
                for low in range(GROUP):
                    base = ((pos[0] % GROUP) ^ low) * span
                    for i in range(row_local):
                        start = pl.multiple_of(base + i * RANK, RANK)
                        outs[high * GROUP + low][0, i, to] = stage[pl.ds(start, RANK)]


def project(pos, col_factors, wavefield, piece, chunk, width, tiles, split, base, groups, after):
    first, freqs = piece
    _, _, src_rows, cols = col_factors.shape
    col_local = src_rows // TS
    row_local = cols // RANK // tiles
    lanes = GROUP * row_local * RANK
    shape = (freqs, row_local, col_local * RANK, 2 * width)
    if split:
        out_specs = [pl.BlockSpec((1,) + shape[1:], lambda f, g, s: (f, 0, 0, 0))] * (groups * GROUP)
        out_shape = [jax.ShapeDtypeStruct(shape, jnp.bfloat16)] * (groups * GROUP)
    else:
        out_specs = pl.BlockSpec((GROUP, 1) + shape[1:], lambda f, g, s: (g, f, 0, 0, 0))
        out_shape = jax.ShapeDtypeStruct((tiles,) + shape, jnp.bfloat16)
    return call(
        functools.partial(project_kernel, (groups, col_local, row_local, width, split)),
        (freqs, groups),
        1,
        [
            pl.BlockSpec(
                (1, 2, src_rows, lanes),
                lambda f, g, s: (first + f, 0, 0, (s[0] // GROUP) ^ (base + g) if split else g),
            ),
            pl.BlockSpec((1, 2, src_rows, width), lambda f, g, s: (first + f, 0, 0, chunk)),
        ],
        out_specs,
        out_shape,
        [pltpu.VMEM((2 * width, src_rows), jnp.bfloat16)]
        + [pltpu.VMEM((lanes, 2 * width), jnp.bfloat16)] * split,
        8 * freqs * src_rows * groups * lanes * width,
        freqs * 4 * src_rows * (groups * lanes + 2 * width),
        after,
    )(pos, col_factors, wavefield)


def gather(pos, got, step, stage):
    if stage is None:
        return got[0][:, 0, 0].reshape(-1, got[0].shape[-1])
    for m, ref in enumerate(got):
        stage[pl.ds(pl.multiple_of((pos[0] ^ m) * step, step), step)] = ref[0, 0]
    return stage[...]


def expand_kernel(dims, pos, u_ref, *refs):
    count, shares, step, width = dims
    got, outs, stage = refs[:count], refs[count : count + shares], refs[count + shares]
    coeffs = gather(pos, got, step, refs[-1] if count > 1 else None)
    with_real = dot(u_ref[0, 0], coeffs)
    with_imag = dot(u_ref[0, 1], coeffs)
    stage[:, :width] = (with_real[:, :width] - with_imag[:, width:]).astype(jnp.bfloat16)
    stage[:, width:] = (with_real[:, width:] + with_imag[:, :width]).astype(jnp.bfloat16)
    share = TS // shares
    for g in range(shares):
        rows = pl.ds(pl.multiple_of((pos[1] ^ g) * share, share), share)
        outs[g][0, 0] = stage[rows]


def gather_specs(got, index):
    step, both = got[0].shape[-2:]
    if len(got) == 1:
        return [pl.BlockSpec((got[0].shape[0], 1, 1, step, both), lambda *n: (0,) + index(*n))], []
    stage = pltpu.VMEM((len(got) * step, both), got[0].dtype)
    return [pl.BlockSpec((1, 1, step, both), index)] * len(got), [stage]


def expand(pos, row_factors, piece, got, shares, after):
    first, freqs = piece
    _, _, rec_rows, cols = row_factors.shape
    row_local = rec_rows // TS
    step, both = got[0].shape[-2:]
    shape = (freqs, row_local, TS // shares, both)
    specs, scratch = gather_specs(got, lambda f, i, s: (f, i, 0, 0))
    return call(
        functools.partial(expand_kernel, (len(got), shares, step, both // 2)),
        (freqs, row_local),
        1,
        [pl.BlockSpec((1, 2, TS, cols), lambda f, i, s: (first + f, 0, i, 0))] + specs,
        [pl.BlockSpec((1, 1, TS // shares, both), lambda f, i, s: (f, i, 0, 0))] * shares,
        [jax.ShapeDtypeStruct(shape, jnp.bfloat16)] * shares,
        [pltpu.VMEM((TS, both), jnp.bfloat16)] + scratch,
        4 * freqs * rec_rows * cols * both,
        freqs * 2 * (rec_rows * (2 * cols + both) + row_local * cols * both),
        after,
    )(pos, row_factors, *got)


def window_kernel(dims, cosine, sine, index_ref, *refs):
    shares, took, gave, rows, slab, width = dims
    ins, outs = refs[: shares * len(took)], refs[shares * len(took) :]
    half = NT // 2
    masks = [t < index_ref[...] for t in range(NT)]

    def planes(arrays, pieces):
        return [
            (arrays[p * shares + g], f)
            for g in range(shares)
            for p, (_, freqs) in enumerate(pieces)
            for f in range(freqs)
        ]

    def body(n, carry):
        at = pl.ds(pl.multiple_of(n * slab, slab), slab)
        real = [ref[f, 0, at, :width].astype(jnp.float32) for ref, f in planes(ins, took)]
        imag = [ref[f, 0, at, width:].astype(jnp.float32) for ref, f in planes(ins, took)]
        count = len(real)
        even = [sum(cosine[t, k] * real[k] for k in range(count)) for t in range(half)]
        odd = [None] + [sum(sine[t, k] * imag[k] for k in range(count)) for t in range(1, half + 1)]
        zero = jnp.zeros_like(real[0])

        def keep(t, value):
            return jnp.where(masks[t], value, zero)

        diff = [keep(0, even[0])]
        total = [None]
        for t in range(1, half):
            one = keep(t, even[t] - odd[t])
            other = keep(NT - t, -even[t] - odd[t])
            diff.append(one - other)
            total.append(one + other)
        total.append(keep(half, -odd[half]))
        for k, (ref, f) in enumerate(planes(outs, gave)):
            out = sum(cosine[t, k] * diff[t] for t in range(half))
            ref[f, 0, at, :width] = out.astype(jnp.bfloat16)
            out = -sum(sine[t, k] * total[t] for t in range(1, half + 1))
            ref[f, 0, at, width:] = out.astype(jnp.bfloat16)
        return carry

    lax.fori_loop(0, rows // slab, body, 0)


def window(cosine, sine, index, parts, took, gave, chunk):
    shares = len(parts[0])
    _, row_local, rows, both = parts[0][0].shape

    def spec(freqs):
        return pl.BlockSpec((freqs, 1, rows, both), lambda i, c, s: (0, i, 0, 0))

    size = sum(part.size for group in parts for part in group)
    made = call(
        functools.partial(window_kernel, (shares, took, gave, rows, 16, both // 2)),
        (row_local,),
        2,
        [pl.BlockSpec((1, both // 2), lambda i, c, s: (0, chunk))]
        + [spec(freqs) for _, freqs in took for _ in range(shares)],
        [spec(freqs) for _, freqs in gave for _ in range(shares)],
        [
            jax.ShapeDtypeStruct((freqs, row_local, rows, both), jnp.bfloat16)
            for _, freqs in gave
            for _ in range(shares)
        ],
        [],
        2 * NT * size,
        4 * size,
        None,
    )(cosine, sine, index, *[part for group in parts for part in group])
    return [made[p * shares : (p + 1) * shares] for p in range(len(gave))]


def contract_kernel(dims, pos, u_ref, *refs):
    tiles, shares, col_local, width, split = dims
    ins, outs = refs[:shares], refs[shares : shares + (tiles if split else 1)]
    stage = refs[shares + len(outs)]
    share = TS // shares
    for g in range(shares):
        stage[pl.ds(pl.multiple_of((pos[1] ^ g) * share, share), share)] = ins[g][0, 0]
    with_real = turned(stage[...], u_ref[0, 0])
    with_imag = turned(stage[...], u_ref[0, 1])
    real = with_real[:width] + with_imag[width:]
    imag = with_real[width:] - with_imag[:width]
    both = jnp.concatenate([real, imag], 0).astype(jnp.bfloat16).T
    if not split:
        outs[0][:, 0] = both.reshape(tiles, col_local, RANK, 2 * width)
        return
    rows = refs[-1]
    rows[...] = both
    for m in range(tiles):
        for c in range(col_local):
            start = ((pos[0] ^ m) * col_local + c) * RANK
            outs[m][0, c] = rows[pl.ds(pl.multiple_of(start, RANK), RANK)]


def contract(pos, row_factors, piece, parts, tiles, split, after):
    first, freqs = piece
    _, _, rec_rows, cols = row_factors.shape
    row_local = rec_rows // TS
    shares = len(parts)
    share, both = parts[0].shape[2:]
    col_local = cols // RANK // tiles
    shape = (freqs, col_local, row_local * RANK, both)
    if split:
        out_specs = [pl.BlockSpec((1, col_local, RANK, both), lambda f, i, s: (f, 0, i, 0))] * tiles
        out_shape = [jax.ShapeDtypeStruct(shape, jnp.bfloat16)] * tiles
    else:
        out_specs = pl.BlockSpec((tiles, 1, col_local, RANK, both), lambda f, i, s: (0, f, 0, i, 0))
        out_shape = jax.ShapeDtypeStruct((tiles,) + shape, jnp.bfloat16)
    return call(
        functools.partial(contract_kernel, (tiles, shares, col_local, both // 2, split)),
        (freqs, row_local),
        1,
        [pl.BlockSpec((1, 2, TS, cols), lambda f, i, s: (first + f, 0, i, 0))]
        + [pl.BlockSpec((1, 1, share, both), lambda f, i, s: (f, i, 0, 0))] * shares,
        out_specs,
        out_shape,
        [pltpu.VMEM((TS, both), jnp.bfloat16)] + [pltpu.VMEM((cols, both), jnp.bfloat16)] * split,
        4 * freqs * rec_rows * cols * both,
        freqs * 2 * (rec_rows * (2 * cols + both) + row_local * cols * both),
        after,
    )(pos, row_factors, *parts)


def spread_kernel(dims, pos, v_ref, *refs):
    count, carried, step, width = dims
    got, out = refs[:count], refs[count + carried]
    coeffs = gather(pos, got, step, refs[-1] if count > 1 else None)
    with_real = dot(v_ref[0, 0], coeffs)
    with_imag = dot(v_ref[0, 1], coeffs)
    out[0, 0] = with_real[:, :width] - with_imag[:, width:]
    out[0, 1] = with_real[:, width:] + with_imag[:, :width]


def spread(pos, col_factors, piece, got, chunk, points, before, after):
    first, freqs = piece
    total, _, src_rows, cols = col_factors.shape
    step, both = got[0].shape[-2:]
    carried = 0 if before is None else 1
    specs, scratch = gather_specs(got, lambda f, c, s: (f, c, 0, 0))
    return call(
        functools.partial(spread_kernel, (len(got), carried, step, both // 2)),
        (freqs, src_rows // TS),
        1,
        [pl.BlockSpec((1, 2, TS, cols), lambda f, c, s: (first + f, 0, c, 0))]
        + specs
        + [pl.BlockSpec(memory_space=pl.ANY)] * carried,
        pl.BlockSpec((1, 2, TS, both // 2), lambda f, c, s: (first + f, 0, c, chunk)),
        jax.ShapeDtypeStruct((total, 2, src_rows, points), jnp.float32),
        scratch,
        4 * freqs * src_rows * cols * both,
        freqs * 4 * (src_rows * (cols + both) + cols * both),
        after,
        input_output_aliases={2 + len(got): 0} if carried else {},
    )(pos, col_factors, *got, *([before] if carried else []))


def send(array, axis, size, mask):
    if mask == 0:
        return array
    return lax.ppermute(array, axis, [(n, n ^ mask) for n in range(size)])


def trade(made, tiles, split):
    if not split:
        return [lax.all_to_all(made, "tile", 0, 0, tiled=True)]
    got = list(made)
    for m in reversed(range(tiles)):
        got[m] = send(made[m], "tile", tiles, m)
    return got


def local(tiles, shares, wavefield, row_factors, col_factors, window_index):
    freqs = wavefield.shape[0]
    points = wavefield.shape[3]
    width = points // CHUNKS
    share = lax.axis_index("freq")
    pos = jnp.stack([lax.axis_index("tile"), share]).astype(jnp.int32)
    owners = share ^ lax.iota(jnp.int32, shares)
    ids = (owners[:, None] * freqs + lax.iota(jnp.int32, freqs)[None, :]).reshape(-1)
    phases = angles(ids)
    cosine = 0.25 * jnp.cos(phases)
    sine = 0.25 * jnp.sin(phases)
    index = window_index.reshape(1, points)

    took = gave = [((0, freqs, False),)] * CHUNKS
    if freqs > 2:
        took = [((0, 1, True), (1, freqs - 1, False))] + took[1:]
        gave = gave[:-1] + [((0, 1, True), (1, freqs - 2, False), (freqs - 1, 1, True))]

    def runs(pieces):
        return tuple(piece[:2] for piece in pieces)

    sent = []
    token = None
    for h in range(CHUNKS):
        sent.append([])
        for *piece, split in took[h]:
            groups = tiles // GROUP
            half = groups // 2 if split else groups
            made = []
            for base in reversed(range(0, groups, half)):
                part = project(
                    pos, col_factors, wavefield, piece, h, width, tiles, split, base, half, token
                )
                token = part[0] if split else part
                made = [part] + made
            made = [*made[0], *made[1]] if split else made[0]
            sent[h].append(trade(made, tiles, split))
    back = []
    for h in range(CHUNKS):
        parts = []
        for n, (*piece, split) in enumerate(took[h]):
            made = expand(pos, row_factors, piece, sent[h][n], shares, token)
            token = made[0]
            parts.append([send(part, "freq", shares, m) for m, part in enumerate(made)])
        parts = window(cosine, sine, index, parts, runs(took[h]), runs(gave[h]), h)
        parts = [[send(part, "freq", shares, m) for m, part in enumerate(group)] for group in parts]
        back.append([])
        token = None
        for n, (*piece, split) in enumerate(gave[h]):
            if n == 2:
                token = back[h - 1][0][0]
            made = contract(pos, row_factors, piece, parts[n], tiles, split, token)
            token = made[0] if split else made
            back[h].append(trade(made, tiles, split))
    result = None
    for h in range(CHUNKS):
        for n, (*piece, split) in enumerate(gave[h]):
            result = spread(pos, col_factors, piece, back[h][n], h, points, result, token)
            token = None
    return result


def solution(mesh):
    spec = P("freq", None, "tile", None)
    body = functools.partial(local, mesh.shape["tile"], mesh.shape["freq"])
    return jax.shard_map(
        body, mesh=mesh, in_specs=(spec, spec, spec, P()), out_specs=spec, check_vma=False
    )
```

```python
import functools
import math

import jax
import jax.numpy as jnp
from jax import lax
from jax.experimental import pallas as pl
from jax.experimental.pallas import tpu as pltpu
from jax.sharding import PartitionSpec as P


TS = 512
RANK = 32
NT = 16
CHUNKS = 2
GROUP = 4
VMEM_BYTES = 67043328


def angles(freq_ids):
    times = lax.broadcasted_iota(jnp.int32, (NT, freq_ids.shape[0]), 0)
    return math.pi / NT * ((2 * freq_ids[None, :] + 1) * times).astype(jnp.float32)


def call(kernel, grid, prefetch, in_specs, out_specs, out_shape, scratch, flops, nbytes, after, **kw):
    count = prefetch + len(in_specs)
    inner = kernel
    if after is not None:
        in_specs = in_specs + [pl.BlockSpec(memory_space=pl.ANY)]

        def inner(*refs):
            kernel(*refs[:count], *refs[count + 1 :])

    made = pl.pallas_call(
        inner,
        grid_spec=pltpu.PrefetchScalarGridSpec(
            num_scalar_prefetch=prefetch,
            grid=grid,
            in_specs=in_specs,
            out_specs=out_specs,
            scratch_shapes=scratch,
        ),
        out_shape=out_shape,
        cost_estimate=pl.CostEstimate(flops=flops, bytes_accessed=nbytes, transcendentals=0),
        compiler_params=pltpu.CompilerParams(vmem_limit_bytes=VMEM_BYTES),
        **kw,
    )
    return made if after is None else lambda *args: made(*args, after)


def dot(left, right):
    return jnp.dot(left, right, preferred_element_type=jnp.float32)


def turned(left, right):
    return lax.dot_general(left, right, (((0,), (0,)), ((), ())), preferred_element_type=jnp.float32)


def project_kernel(dims, pos, v_ref, w_ref, *refs):
    groups, col_local, row_local, width, split = dims
    span = row_local * RANK
    outs = refs[: groups * GROUP if split else 1]
    wave = refs[len(outs)]

    @pl.when(pl.program_id(1) == 0)
    def _():
        wave[:width] = w_ref[0, 0].T
        wave[width:] = w_ref[0, 1].T

    for c in range(col_local):
        rows = slice(c * TS, (c + 1) * TS)
        to = slice(c * RANK, (c + 1) * RANK)
        with_real = dot(wave[:, rows], v_ref[0, 0, rows])
        with_imag = dot(wave[:, rows], v_ref[0, 1, rows])
        real = with_real[:width] + with_imag[width:]
        imag = with_real[width:] - with_imag[:width]
        both = jnp.concatenate([real, imag], 0).astype(jnp.bfloat16).T
        if not split:
            for d in range(GROUP):
                for i in range(row_local):
                    start = d * span + i * RANK
                    outs[0][d, 0, i, to] = both[start : start + RANK]
            continue
        stage = refs[-1]
        stage[...] = both
        for high in range(groups):

            @pl.when(pl.program_id(1) == high)
            def _():
                for low in range(GROUP):
                    base = ((pos[0] % GROUP) ^ low) * span
                    for i in range(row_local):
                        start = pl.multiple_of(base + i * RANK, RANK)
                        outs[high * GROUP + low][0, i, to] = stage[pl.ds(start, RANK)]


def project(pos, col_factors, wavefield, piece, chunk, width, tiles, split, base, groups, after):
    first, freqs = piece
    _, _, src_rows, cols = col_factors.shape
    col_local = src_rows // TS
    row_local = cols // RANK // tiles
    lanes = GROUP * row_local * RANK
    shape = (freqs, row_local, col_local * RANK, 2 * width)
    if split:
        out_specs = [pl.BlockSpec((1,) + shape[1:], lambda f, g, s: (f, 0, 0, 0))] * (groups * GROUP)
        out_shape = [jax.ShapeDtypeStruct(shape, jnp.bfloat16)] * (groups * GROUP)
    else:
        out_specs = pl.BlockSpec((GROUP, 1) + shape[1:], lambda f, g, s: (g, f, 0, 0, 0))
        out_shape = jax.ShapeDtypeStruct((tiles,) + shape, jnp.bfloat16)
    return call(
        functools.partial(project_kernel, (groups, col_local, row_local, width, split)),
        (freqs, groups),
        1,
        [
            pl.BlockSpec(
                (1, 2, src_rows, lanes),
                lambda f, g, s: (first + f, 0, 0, (s[0] // GROUP) ^ (base + g) if split else g),
            ),
            pl.BlockSpec((1, 2, src_rows, width), lambda f, g, s: (first + f, 0, 0, chunk)),
        ],
        out_specs,
        out_shape,
        [pltpu.VMEM((2 * width, src_rows), jnp.bfloat16)]
        + [pltpu.VMEM((lanes, 2 * width), jnp.bfloat16)] * split,
        8 * freqs * src_rows * groups * lanes * width,
        freqs * 4 * src_rows * (groups * lanes + 2 * width),
        after,
    )(pos, col_factors, wavefield)


def gather(pos, got, step, stage):
    if stage is None:
        return got[0][:, 0, 0].reshape(-1, got[0].shape[-1])
    for m, ref in enumerate(got):
        stage[pl.ds(pl.multiple_of((pos[0] ^ m) * step, step), step)] = ref[0, 0]
    return stage[...]


def expand_kernel(dims, pos, u_ref, *refs):
    count, shares, step, width = dims
    got, outs, stage = refs[:count], refs[count : count + shares], refs[count + shares]
    coeffs = gather(pos, got, step, refs[-1] if count > 1 else None)
    with_real = dot(u_ref[0, 0], coeffs)
    with_imag = dot(u_ref[0, 1], coeffs)
    stage[:, :width] = (with_real[:, :width] - with_imag[:, width:]).astype(jnp.bfloat16)
    stage[:, width:] = (with_real[:, width:] + with_imag[:, :width]).astype(jnp.bfloat16)
    share = TS // shares
    for g in range(shares):
        rows = pl.ds(pl.multiple_of((pos[1] ^ g) * share, share), share)
        outs[g][0, 0] = stage[rows]


def gather_specs(got, index):
    step, both = got[0].shape[-2:]
    if len(got) == 1:
        return [pl.BlockSpec((got[0].shape[0], 1, 1, step, both), lambda *n: (0,) + index(*n))], []
    stage = pltpu.VMEM((len(got) * step, both), got[0].dtype)
    return [pl.BlockSpec((1, 1, step, both), index)] * len(got), [stage]


def expand(pos, row_factors, piece, got, shares, after):
    first, freqs = piece
    _, _, rec_rows, cols = row_factors.shape
    row_local = rec_rows // TS
    step, both = got[0].shape[-2:]
    shape = (freqs, row_local, TS // shares, both)
    specs, scratch = gather_specs(got, lambda f, i, s: (f, i, 0, 0))
    return call(
        functools.partial(expand_kernel, (len(got), shares, step, both // 2)),
        (freqs, row_local),
        1,
        [pl.BlockSpec((1, 2, TS, cols), lambda f, i, s: (first + f, 0, i, 0))] + specs,
        [pl.BlockSpec((1, 1, TS // shares, both), lambda f, i, s: (f, i, 0, 0))] * shares,
        [jax.ShapeDtypeStruct(shape, jnp.bfloat16)] * shares,
        [pltpu.VMEM((TS, both), jnp.bfloat16)] + scratch,
        4 * freqs * rec_rows * cols * both,
        freqs * 2 * (rec_rows * (2 * cols + both) + row_local * cols * both),
        after,
    )(pos, row_factors, *got)


def window_kernel(dims, cosine, sine, index_ref, *refs):
    shares, took, gave, rows, slab, width = dims
    ins, outs = refs[: shares * len(took)], refs[shares * len(took) :]
    half = NT // 2
    masks = [t < index_ref[...] for t in range(NT)]

    def planes(arrays, pieces):
        return [
            (arrays[p * shares + g], f)
            for g in range(shares)
            for p, (_, freqs) in enumerate(pieces)
            for f in range(freqs)
        ]

    def body(n, carry):
        at = pl.ds(pl.multiple_of(n * slab, slab), slab)
        real = [ref[f, 0, at, :width].astype(jnp.float32) for ref, f in planes(ins, took)]
        imag = [ref[f, 0, at, width:].astype(jnp.float32) for ref, f in planes(ins, took)]
        count = len(real)
        even = [sum(cosine[t, k] * real[k] for k in range(count)) for t in range(half)]
        odd = [None] + [sum(sine[t, k] * imag[k] for k in range(count)) for t in range(1, half + 1)]
        zero = jnp.zeros_like(real[0])

        def keep(t, value):
            return jnp.where(masks[t], value, zero)

        diff = [keep(0, even[0])]
        total = [None]
        for t in range(1, half):
            one = keep(t, even[t] - odd[t])
            other = keep(NT - t, -even[t] - odd[t])
            diff.append(one - other)
            total.append(one + other)
        total.append(keep(half, -odd[half]))
        for k, (ref, f) in enumerate(planes(outs, gave)):
            out = sum(cosine[t, k] * diff[t] for t in range(half))
            ref[f, 0, at, :width] = out.astype(jnp.bfloat16)
            out = -sum(sine[t, k] * total[t] for t in range(1, half + 1))
            ref[f, 0, at, width:] = out.astype(jnp.bfloat16)
        return carry

    lax.fori_loop(0, rows // slab, body, 0)


def window(cosine, sine, index, parts, took, gave, chunk):
    shares = len(parts[0])
    _, row_local, rows, both = parts[0][0].shape

    def spec(freqs):
        return pl.BlockSpec((freqs, 1, rows, both), lambda i, c, s: (0, i, 0, 0))

    size = sum(part.size for group in parts for part in group)
    made = call(
        functools.partial(window_kernel, (shares, took, gave, rows, 16, both // 2)),
        (row_local,),
        2,
        [pl.BlockSpec((1, both // 2), lambda i, c, s: (0, chunk))]
        + [spec(freqs) for _, freqs in took for _ in range(shares)],
        [spec(freqs) for _, freqs in gave for _ in range(shares)],
        [
            jax.ShapeDtypeStruct((freqs, row_local, rows, both), jnp.bfloat16)
            for _, freqs in gave
            for _ in range(shares)
        ],
        [],
        2 * NT * size,
        4 * size,
        None,
    )(cosine, sine, index, *[part for group in parts for part in group])
    return [made[p * shares : (p + 1) * shares] for p in range(len(gave))]


def contract_kernel(dims, pos, u_ref, *refs):
    tiles, shares, col_local, width, split = dims
    ins, outs = refs[:shares], refs[shares : shares + (tiles if split else 1)]
    stage = refs[shares + len(outs)]
    share = TS // shares
    for g in range(shares):
        stage[pl.ds(pl.multiple_of((pos[1] ^ g) * share, share), share)] = ins[g][0, 0]
    with_real = turned(stage[...], u_ref[0, 0])
    with_imag = turned(stage[...], u_ref[0, 1])
    real = with_real[:width] + with_imag[width:]
    imag = with_real[width:] - with_imag[:width]
    both = jnp.concatenate([real, imag], 0).astype(jnp.bfloat16).T
    if not split:
        outs[0][:, 0] = both.reshape(tiles, col_local, RANK, 2 * width)
        return
    rows = refs[-1]
    rows[...] = both
    for m in range(tiles):
        for c in range(col_local):
            start = ((pos[0] ^ m) * col_local + c) * RANK
            outs[m][0, c] = rows[pl.ds(pl.multiple_of(start, RANK), RANK)]


def contract(pos, row_factors, piece, parts, tiles, split, after):
    first, freqs = piece
    _, _, rec_rows, cols = row_factors.shape
    row_local = rec_rows // TS
    shares = len(parts)
    share, both = parts[0].shape[2:]
    col_local = cols // RANK // tiles
    shape = (freqs, col_local, row_local * RANK, both)
    if split:
        out_specs = [pl.BlockSpec((1, col_local, RANK, both), lambda f, i, s: (f, 0, i, 0))] * tiles
        out_shape = [jax.ShapeDtypeStruct(shape, jnp.bfloat16)] * tiles
    else:
        out_specs = pl.BlockSpec((tiles, 1, col_local, RANK, both), lambda f, i, s: (0, f, 0, i, 0))
        out_shape = jax.ShapeDtypeStruct((tiles,) + shape, jnp.bfloat16)
    return call(
        functools.partial(contract_kernel, (tiles, shares, col_local, both // 2, split)),
        (freqs, row_local),
        1,
        [pl.BlockSpec((1, 2, TS, cols), lambda f, i, s: (first + f, 0, i, 0))]
        + [pl.BlockSpec((1, 1, share, both), lambda f, i, s: (f, i, 0, 0))] * shares,
        out_specs,
        out_shape,
        [pltpu.VMEM((TS, both), jnp.bfloat16)] + [pltpu.VMEM((cols, both), jnp.bfloat16)] * split,
        4 * freqs * rec_rows * cols * both,
        freqs * 2 * (rec_rows * (2 * cols + both) + row_local * cols * both),
        after,
    )(pos, row_factors, *parts)


def spread_kernel(dims, pos, v_ref, *refs):
    count, carried, step, width = dims
    got, out = refs[:count], refs[count + carried]
    coeffs = gather(pos, got, step, refs[-1] if count > 1 else None)
    with_real = dot(v_ref[0, 0], coeffs)
    with_imag = dot(v_ref[0, 1], coeffs)
    out[0, 0] = with_real[:, :width] - with_imag[:, width:]
    out[0, 1] = with_real[:, width:] + with_imag[:, :width]


def spread(pos, col_factors, piece, got, chunk, points, before, after):
    first, freqs = piece
    total, _, src_rows, cols = col_factors.shape
    step, both = got[0].shape[-2:]
    carried = 0 if before is None else 1
    specs, scratch = gather_specs(got, lambda f, c, s: (f, c, 0, 0))
    return call(
        functools.partial(spread_kernel, (len(got), carried, step, both // 2)),
        (freqs, src_rows // TS),
        1,
        [pl.BlockSpec((1, 2, TS, cols), lambda f, c, s: (first + f, 0, c, 0))]
        + specs
        + [pl.BlockSpec(memory_space=pl.ANY)] * carried,
        pl.BlockSpec((1, 2, TS, both // 2), lambda f, c, s: (first + f, 0, c, chunk)),
        jax.ShapeDtypeStruct((total, 2, src_rows, points), jnp.float32),
        scratch,
        4 * freqs * src_rows * cols * both,
        freqs * 4 * (src_rows * (cols + both) + cols * both),
        after,
        input_output_aliases={2 + len(got): 0} if carried else {},
    )(pos, col_factors, *got, *([before] if carried else []))


def finish_kernel(dims, pos, *refs):
    groups, step, width, adds = dims
    held, got = refs[:groups], refs[groups : groups * (1 + GROUP)]
    out, stage = refs[-2:]
    with_real = with_imag = 0.0
    for n, v_ref in enumerate(held):
        for seat in range(GROUP):
            row = ((pos[0] % GROUP) ^ seat) * step
            stage[n, pl.ds(pl.multiple_of(row, step), step)] = got[n * GROUP + seat][0, 0]
        with_real = with_real + dot(v_ref[0, 0], stage[n])
        with_imag = with_imag + dot(v_ref[0, 1], stage[n])
    real = with_real[:, :width] - with_imag[:, width:]
    imag = with_real[:, width:] + with_imag[:, :width]
    if adds:
        part = refs[groups * (1 + GROUP)]
        real, imag = part[0, 0] + real, part[0, 1] + imag
    out[0, 0] = real
    out[0, 1] = imag


def finish(pos, col_factors, piece, got, highs, chunk, points, part, before, after):
    first, freqs = piece
    total, _, src_rows, _ = col_factors.shape
    step, both = got[0].shape[-2:]
    width, groups = both // 2, len(highs)
    own = pl.BlockSpec((1, 2, TS, width), lambda f, c, s: (f, 0, c, 0))
    last = before is not None
    adds = part is not None
    shape = (total, 2, src_rows, points) if last else (freqs, 2, src_rows, width)

    def held(high):
        return pl.BlockSpec(
            (1, 2, TS, GROUP * step), lambda f, c, s: (first + f, 0, c, (s[0] // GROUP) ^ high)
        )

    return call(
        functools.partial(finish_kernel, (groups, step, width, adds)),
        (freqs, src_rows // TS),
        1,
        [held(high) for high in highs]
        + [pl.BlockSpec((1, 1, step, both), lambda f, c, s: (f, c, 0, 0))] * len(got)
        + [own] * adds
        + [pl.BlockSpec(memory_space=pl.ANY)] * last,
        pl.BlockSpec((1, 2, TS, width), lambda f, c, s: (first + f, 0, c, chunk)) if last else own,
        jax.ShapeDtypeStruct(shape, jnp.float32),
        [pltpu.VMEM((groups, GROUP * step, both), got[0].dtype)],
        4 * freqs * src_rows * len(got) * step * both,
        freqs * 4 * (src_rows * (len(got) * step + both) + len(got) * step * both),
        after,
        input_output_aliases={1 + groups + len(got) + adds: 0} if last else {},
    )(pos, *[col_factors] * groups, *got, *([part] if adds else []), *([before] if last else []))


def send(array, axis, size, mask):
    if mask == 0:
        return array
    return lax.ppermute(array, axis, [(n, n ^ mask) for n in range(size)])


def trade(made, tiles, split):
    if not split:
        return [lax.all_to_all(made, "tile", 0, 0, tiled=True)]
    got = list(made)
    for m in reversed(range(tiles)):
        got[m] = send(made[m], "tile", tiles, m)
    return got


def local(tiles, shares, wavefield, row_factors, col_factors, window_index):
    freqs = wavefield.shape[0]
    points = wavefield.shape[3]
    width = points // CHUNKS
    share = lax.axis_index("freq")
    pos = jnp.stack([lax.axis_index("tile"), share]).astype(jnp.int32)
    owners = share ^ lax.iota(jnp.int32, shares)
    ids = (owners[:, None] * freqs + lax.iota(jnp.int32, freqs)[None, :]).reshape(-1)
    phases = angles(ids)
    cosine = 0.25 * jnp.cos(phases)
    sine = 0.25 * jnp.sin(phases)
    index = window_index.reshape(1, points)

    took = gave = [((0, freqs, False),)] * CHUNKS
    if freqs > 2:
        took = [((0, freqs - 1, False), (freqs - 1, 1, True))] * CHUNKS
        took = [((0, 1, True), (1, freqs - 2, False), (freqs - 1, 1, True))] + took[1:]
        gave = gave[:-1] + [((0, 1, True), (1, freqs - 2, False), (freqs - 1, 1, True))]

    def runs(pieces):
        return tuple(piece[:2] for piece in pieces)

    sent = []
    token = None
    for h in range(CHUNKS):
        sent.append([])
        for n, (*piece, split) in enumerate(took[h]):
            groups = tiles // GROUP
            some = 1 if split and h == n == 0 else groups
            made = []
            for base in reversed(range(0, groups, some)):
                part = project(
                    pos, col_factors, wavefield, piece, h, width, tiles, split, base, some, token
                )
                token = part[0] if split else part
                made = [*part, *made] if split else part
            sent[h].append(trade(made, tiles, split))
    back = []
    for h in range(CHUNKS):
        parts = []
        for n, (*piece, split) in enumerate(took[h]):
            made = expand(pos, row_factors, piece, sent[h][n], shares, token)
            token = made[0]
            parts.append([send(part, "freq", shares, m) for m, part in enumerate(made)])
        parts = window(cosine, sine, index, parts, runs(took[h]), runs(gave[h]), h)
        parts = [
            [send(part, "freq", shares, m) for m, part in enumerate(group)] for group in parts
        ]
        back.append([])
        token = None
        for n, (*piece, split) in enumerate(gave[h]):
            if n == 2:
                token = back[h - 1][0][0]
            made = contract(pos, row_factors, piece, parts[n], tiles, split, token)
            token = made[0] if split else made
            back[h].append(trade(made, tiles, split))
    result = None
    for h in range(CHUNKS):
        for n, (*piece, split) in enumerate(gave[h]):
            if n == 2:
                slow = tiles // GROUP // 2
                most = tuple(high for high in range(tiles // GROUP) if high != slow)
                part = None
                for highs in (most, (slow,)):
                    group = [back[h][n][high * GROUP + seat] for high in highs for seat in range(GROUP)]
                    ends = part is not None
                    part = finish(
                        pos, col_factors, piece, group, highs, h, points, part,
                        result if ends else None, None if ends else result,
                    )
                result = part
                continue
            result = spread(pos, col_factors, piece, back[h][n], h, points, result, token)
            token = None
    return result


def solution(mesh):
    spec = P("freq", None, "tile", None)
    body = functools.partial(local, mesh.shape["tile"], mesh.shape["freq"])
    return jax.shard_map(
        body, mesh=mesh, in_specs=(spec, spec, spec, P()), out_specs=spec, check_vma=False
    )
```

```python
import functools
import math

import jax
import jax.numpy as jnp
from jax import lax
from jax.experimental import pallas as pl
from jax.experimental.pallas import tpu as pltpu
from jax.sharding import PartitionSpec as P


TS = 512
RANK = 32
NT = 16
CHUNKS = 2
GROUP = 4
VMEM_BYTES = 67043328


def angles(freq_ids):
    times = lax.broadcasted_iota(jnp.int32, (NT, freq_ids.shape[0]), 0)
    return math.pi / NT * ((2 * freq_ids[None, :] + 1) * times).astype(jnp.float32)


def call(kernel, grid, prefetch, in_specs, out_specs, out_shape, scratch, flops, nbytes, after, **kw):
    count = prefetch + len(in_specs)
    inner = kernel
    if after is not None:
        in_specs = in_specs + [pl.BlockSpec(memory_space=pl.ANY)]

        def inner(*refs):
            kernel(*refs[:count], *refs[count + 1 :])

    made = pl.pallas_call(
        inner,
        grid_spec=pltpu.PrefetchScalarGridSpec(
            num_scalar_prefetch=prefetch,
            grid=grid,
            in_specs=in_specs,
            out_specs=out_specs,
            scratch_shapes=scratch,
        ),
        out_shape=out_shape,
        cost_estimate=pl.CostEstimate(flops=flops, bytes_accessed=nbytes, transcendentals=0),
        compiler_params=pltpu.CompilerParams(vmem_limit_bytes=VMEM_BYTES),
        **kw,
    )
    return made if after is None else lambda *args: made(*args, after)


def dot(left, right):
    return jnp.dot(left, right, preferred_element_type=jnp.float32)


def turned(left, right):
    return lax.dot_general(left, right, (((0,), (0,)), ((), ())), preferred_element_type=jnp.float32)


def project_kernel(dims, pos, v_ref, w_ref, *refs):
    groups, col_local, row_local, width, split = dims
    span = row_local * RANK
    outs = refs[: groups * GROUP if split else 1]
    wave = refs[len(outs)]

    @pl.when(pl.program_id(1) == 0)
    def _():
        wave[:width] = w_ref[0, 0].T
        wave[width:] = w_ref[0, 1].T

    for c in range(col_local):
        rows = slice(c * TS, (c + 1) * TS)
        to = slice(c * RANK, (c + 1) * RANK)
        with_real = dot(wave[:, rows], v_ref[0, 0, rows])
        with_imag = dot(wave[:, rows], v_ref[0, 1, rows])
        real = with_real[:width] + with_imag[width:]
        imag = with_real[width:] - with_imag[:width]
        both = jnp.concatenate([real, imag], 0).astype(jnp.bfloat16).T
        if not split:
            for d in range(GROUP):
                for i in range(row_local):
                    start = d * span + i * RANK
                    outs[0][d, 0, i, to] = both[start : start + RANK]
            continue
        stage = refs[-1]
        stage[...] = both
        for high in range(groups):

            @pl.when(pl.program_id(1) == high)
            def _():
                for low in range(GROUP):
                    base = ((pos[0] % GROUP) ^ low) * span
                    for i in range(row_local):
                        start = pl.multiple_of(base + i * RANK, RANK)
                        outs[high * GROUP + low][0, i, to] = stage[pl.ds(start, RANK)]


def project(pos, col_factors, wavefield, piece, chunk, width, tiles, split, base, groups, after):
    first, freqs = piece
    _, _, src_rows, cols = col_factors.shape
    col_local = src_rows // TS
    row_local = cols // RANK // tiles
    lanes = GROUP * row_local * RANK
    shape = (freqs, row_local, col_local * RANK, 2 * width)
    if split:
        out_specs = [pl.BlockSpec((1,) + shape[1:], lambda f, g, s: (f, 0, 0, 0))] * (groups * GROUP)
        out_shape = [jax.ShapeDtypeStruct(shape, jnp.bfloat16)] * (groups * GROUP)
    else:
        out_specs = pl.BlockSpec((GROUP, 1) + shape[1:], lambda f, g, s: (g, f, 0, 0, 0))
        out_shape = jax.ShapeDtypeStruct((tiles,) + shape, jnp.bfloat16)
    return call(
        functools.partial(project_kernel, (groups, col_local, row_local, width, split)),
        (freqs, groups),
        1,
        [
            pl.BlockSpec(
                (1, 2, src_rows, lanes),
                lambda f, g, s: (first + f, 0, 0, (s[0] // GROUP) ^ (base + g) if split else g),
            ),
            pl.BlockSpec((1, 2, src_rows, width), lambda f, g, s: (first + f, 0, 0, chunk)),
        ],
        out_specs,
        out_shape,
        [pltpu.VMEM((2 * width, src_rows), jnp.bfloat16)]
        + [pltpu.VMEM((lanes, 2 * width), jnp.bfloat16)] * split,
        8 * freqs * src_rows * groups * lanes * width,
        freqs * 4 * src_rows * (groups * lanes + 2 * width),
        after,
    )(pos, col_factors, wavefield)


def gather(pos, got, step, stage):
    if stage is None:
        return got[0][:, 0, 0].reshape(-1, got[0].shape[-1])
    for m, ref in enumerate(got):
        stage[pl.ds(pl.multiple_of((pos[0] ^ m) * step, step), step)] = ref[0, 0]
    return stage[...]


def expand_kernel(dims, pos, u_ref, *refs):
    count, shares, step, width = dims
    got, outs, stage = refs[:count], refs[count : count + shares], refs[count + shares]
    coeffs = gather(pos, got, step, refs[-1] if count > 1 else None)
    with_real = dot(u_ref[0, 0], coeffs)
    with_imag = dot(u_ref[0, 1], coeffs)
    stage[:, :width] = (with_real[:, :width] - with_imag[:, width:]).astype(jnp.bfloat16)
    stage[:, width:] = (with_real[:, width:] + with_imag[:, :width]).astype(jnp.bfloat16)
    share = TS // shares
    for g in range(shares):
        rows = pl.ds(pl.multiple_of((pos[1] ^ g) * share, share), share)
        outs[g][0, 0] = stage[rows]


def gather_specs(got, index):
    step, both = got[0].shape[-2:]
    if len(got) == 1:
        return [pl.BlockSpec((got[0].shape[0], 1, 1, step, both), lambda *n: (0,) + index(*n))], []
    stage = pltpu.VMEM((len(got) * step, both), got[0].dtype)
    return [pl.BlockSpec((1, 1, step, both), index)] * len(got), [stage]


def expand(pos, row_factors, piece, got, shares, after):
    first, freqs = piece
    _, _, rec_rows, cols = row_factors.shape
    row_local = rec_rows // TS
    step, both = got[0].shape[-2:]
    shape = (freqs, row_local, TS // shares, both)
    specs, scratch = gather_specs(got, lambda f, i, s: (f, i, 0, 0))
    return call(
        functools.partial(expand_kernel, (len(got), shares, step, both // 2)),
        (freqs, row_local),
        1,
        [pl.BlockSpec((1, 2, TS, cols), lambda f, i, s: (first + f, 0, i, 0))] + specs,
        [pl.BlockSpec((1, 1, TS // shares, both), lambda f, i, s: (f, i, 0, 0))] * shares,
        [jax.ShapeDtypeStruct(shape, jnp.bfloat16)] * shares,
        [pltpu.VMEM((TS, both), jnp.bfloat16)] + scratch,
        4 * freqs * rec_rows * cols * both,
        freqs * 2 * (rec_rows * (2 * cols + both) + row_local * cols * both),
        after,
    )(pos, row_factors, *got)


def window_kernel(dims, cosine, sine, index_ref, *refs):
    shares, took, gave, rows, slab, width = dims
    ins, outs = refs[: shares * len(took)], refs[shares * len(took) :]
    half = NT // 2
    masks = [t < index_ref[...] for t in range(NT)]

    def planes(arrays, pieces):
        return [
            (arrays[p * shares + g], f)
            for g in range(shares)
            for p, (_, freqs) in enumerate(pieces)
            for f in range(freqs)
        ]

    def body(n, carry):
        at = pl.ds(pl.multiple_of(n * slab, slab), slab)
        real = [ref[f, 0, at, :width].astype(jnp.float32) for ref, f in planes(ins, took)]
        imag = [ref[f, 0, at, width:].astype(jnp.float32) for ref, f in planes(ins, took)]
        count = len(real)
        even = [sum(cosine[t, k] * real[k] for k in range(count)) for t in range(half)]
        odd = [None] + [sum(sine[t, k] * imag[k] for k in range(count)) for t in range(1, half + 1)]
        zero = jnp.zeros_like(real[0])

        def keep(t, value):
            return jnp.where(masks[t], value, zero)

        diff = [keep(0, even[0])]
        total = [None]
        for t in range(1, half):
            one = keep(t, even[t] - odd[t])
            other = keep(NT - t, -even[t] - odd[t])
            diff.append(one - other)
            total.append(one + other)
        total.append(keep(half, -odd[half]))
        for k, (ref, f) in enumerate(planes(outs, gave)):
            out = sum(cosine[t, k] * diff[t] for t in range(half))
            ref[f, 0, at, :width] = out.astype(jnp.bfloat16)
            out = -sum(sine[t, k] * total[t] for t in range(1, half + 1))
            ref[f, 0, at, width:] = out.astype(jnp.bfloat16)
        return carry

    lax.fori_loop(0, rows // slab, body, 0)


def window(cosine, sine, index, parts, took, gave, chunk):
    shares = len(parts[0])
    _, row_local, rows, both = parts[0][0].shape

    def spec(freqs):
        return pl.BlockSpec((freqs, 1, rows, both), lambda i, c, s: (0, i, 0, 0))

    size = sum(part.size for group in parts for part in group)
    made = call(
        functools.partial(window_kernel, (shares, took, gave, rows, 16, both // 2)),
        (row_local,),
        2,
        [pl.BlockSpec((1, both // 2), lambda i, c, s: (0, chunk))]
        + [spec(freqs) for _, freqs in took for _ in range(shares)],
        [spec(freqs) for _, freqs in gave for _ in range(shares)],
        [
            jax.ShapeDtypeStruct((freqs, row_local, rows, both), jnp.bfloat16)
            for _, freqs in gave
            for _ in range(shares)
        ],
        [],
        2 * NT * size,
        4 * size,
        None,
    )(cosine, sine, index, *[part for group in parts for part in group])
    return [made[p * shares : (p + 1) * shares] for p in range(len(gave))]


def contract_kernel(dims, pos, u_ref, *refs):
    tiles, shares, col_local, width, split = dims
    ins, outs = refs[:shares], refs[shares : shares + (tiles if split else 1)]
    stage = refs[shares + len(outs)]
    share = TS // shares
    for g in range(shares):
        stage[pl.ds(pl.multiple_of((pos[1] ^ g) * share, share), share)] = ins[g][0, 0]
    with_real = turned(stage[...], u_ref[0, 0])
    with_imag = turned(stage[...], u_ref[0, 1])
    real = with_real[:width] + with_imag[width:]
    imag = with_real[width:] - with_imag[:width]
    both = jnp.concatenate([real, imag], 0).astype(jnp.bfloat16).T
    if not split:
        outs[0][:, 0] = both.reshape(tiles, col_local, RANK, 2 * width)
        return
    rows = refs[-1]
    rows[...] = both
    for m in range(tiles):
        for c in range(col_local):
            start = ((pos[0] ^ m) * col_local + c) * RANK
            outs[m][0, c] = rows[pl.ds(pl.multiple_of(start, RANK), RANK)]


def contract(pos, row_factors, piece, parts, tiles, split, after):
    first, freqs = piece
    _, _, rec_rows, cols = row_factors.shape
    row_local = rec_rows // TS
    shares = len(parts)
    share, both = parts[0].shape[2:]
    col_local = cols // RANK // tiles
    shape = (freqs, col_local, row_local * RANK, both)
    if split:
        out_specs = [pl.BlockSpec((1, col_local, RANK, both), lambda f, i, s: (f, 0, i, 0))] * tiles
        out_shape = [jax.ShapeDtypeStruct(shape, jnp.bfloat16)] * tiles
    else:
        out_specs = pl.BlockSpec((tiles, 1, col_local, RANK, both), lambda f, i, s: (0, f, 0, i, 0))
        out_shape = jax.ShapeDtypeStruct((tiles,) + shape, jnp.bfloat16)
    return call(
        functools.partial(contract_kernel, (tiles, shares, col_local, both // 2, split)),
        (freqs, row_local),
        1,
        [pl.BlockSpec((1, 2, TS, cols), lambda f, i, s: (first + f, 0, i, 0))]
        + [pl.BlockSpec((1, 1, share, both), lambda f, i, s: (f, i, 0, 0))] * shares,
        out_specs,
        out_shape,
        [pltpu.VMEM((TS, both), jnp.bfloat16)] + [pltpu.VMEM((cols, both), jnp.bfloat16)] * split,
        4 * freqs * rec_rows * cols * both,
        freqs * 2 * (rec_rows * (2 * cols + both) + row_local * cols * both),
        after,
    )(pos, row_factors, *parts)


def spread_kernel(dims, pos, v_ref, *refs):
    count, carried, step, width = dims
    got, out = refs[:count], refs[count + carried]
    coeffs = gather(pos, got, step, refs[-1] if count > 1 else None)
    with_real = dot(v_ref[0, 0], coeffs)
    with_imag = dot(v_ref[0, 1], coeffs)
    out[0, 0] = with_real[:, :width] - with_imag[:, width:]
    out[0, 1] = with_real[:, width:] + with_imag[:, :width]


def spread(pos, col_factors, piece, got, chunk, points, before, after):
    first, freqs = piece
    total, _, src_rows, cols = col_factors.shape
    step, both = got[0].shape[-2:]
    carried = 0 if before is None else 1
    specs, scratch = gather_specs(got, lambda f, c, s: (f, c, 0, 0))
    return call(
        functools.partial(spread_kernel, (len(got), carried, step, both // 2)),
        (freqs, src_rows // TS),
        1,
        [pl.BlockSpec((1, 2, TS, cols), lambda f, c, s: (first + f, 0, c, 0))]
        + specs
        + [pl.BlockSpec(memory_space=pl.ANY)] * carried,
        pl.BlockSpec((1, 2, TS, both // 2), lambda f, c, s: (first + f, 0, c, chunk)),
        jax.ShapeDtypeStruct((total, 2, src_rows, points), jnp.float32),
        scratch,
        4 * freqs * src_rows * cols * both,
        freqs * 4 * (src_rows * (cols + both) + cols * both),
        after,
        input_output_aliases={2 + len(got): 0} if carried else {},
    )(pos, col_factors, *got, *([before] if carried else []))


def finish_kernel(dims, pos, *refs):
    groups, step, width, adds = dims
    held, got = refs[:groups], refs[groups : groups * (1 + GROUP)]
    out, stage = refs[-2:]
    with_real = with_imag = 0.0
    for n, v_ref in enumerate(held):
        for seat in range(GROUP):
            row = ((pos[0] % GROUP) ^ seat) * step
            stage[n, pl.ds(pl.multiple_of(row, step), step)] = got[n * GROUP + seat][0, 0]
        with_real = with_real + dot(v_ref[0, 0], stage[n])
        with_imag = with_imag + dot(v_ref[0, 1], stage[n])
    real = with_real[:, :width] - with_imag[:, width:]
    imag = with_real[:, width:] + with_imag[:, :width]
    if adds:
        part = refs[groups * (1 + GROUP)]
        real, imag = part[0, 0] + real, part[0, 1] + imag
    out[0, 0] = real
    out[0, 1] = imag


def finish(pos, col_factors, piece, got, highs, chunk, points, part, before, after):
    first, freqs = piece
    total, _, src_rows, _ = col_factors.shape
    step, both = got[0].shape[-2:]
    width, groups = both // 2, len(highs)
    own = pl.BlockSpec((1, 2, TS, width), lambda f, c, s: (f, 0, c, 0))
    last = before is not None
    adds = part is not None
    shape = (total, 2, src_rows, points) if last else (freqs, 2, src_rows, width)

    def held(high):
        return pl.BlockSpec(
            (1, 2, TS, GROUP * step), lambda f, c, s: (first + f, 0, c, (s[0] // GROUP) ^ high)
        )

    return call(
        functools.partial(finish_kernel, (groups, step, width, adds)),
        (freqs, src_rows // TS),
        1,
        [held(high) for high in highs]
        + [pl.BlockSpec((1, 1, step, both), lambda f, c, s: (f, c, 0, 0))] * len(got)
        + [own] * adds
        + [pl.BlockSpec(memory_space=pl.ANY)] * last,
        pl.BlockSpec((1, 2, TS, width), lambda f, c, s: (first + f, 0, c, chunk)) if last else own,
        jax.ShapeDtypeStruct(shape, jnp.float32),
        [pltpu.VMEM((groups, GROUP * step, both), got[0].dtype)],
        4 * freqs * src_rows * len(got) * step * both,
        freqs * 4 * (src_rows * (len(got) * step + both) + len(got) * step * both),
        after,
        input_output_aliases={1 + groups + len(got) + adds: 0} if last else {},
    )(pos, *[col_factors] * groups, *got, *([part] if adds else []), *([before] if last else []))


def send(array, axis, size, mask):
    if mask == 0:
        return array
    return lax.ppermute(array, axis, [(n, n ^ mask) for n in range(size)])


def trade(made, tiles, split):
    if not split:
        return [lax.all_to_all(made, "tile", 0, 0, tiled=True)]
    got = list(made)
    for m in reversed(range(tiles)):
        got[m] = send(made[m], "tile", tiles, m)
    return got


def local(tiles, shares, wavefield, row_factors, col_factors, window_index):
    freqs = wavefield.shape[0]
    points = wavefield.shape[3]
    width = points // CHUNKS
    share = lax.axis_index("freq")
    pos = jnp.stack([lax.axis_index("tile"), share]).astype(jnp.int32)
    owners = share ^ lax.iota(jnp.int32, shares)
    ids = (owners[:, None] * freqs + lax.iota(jnp.int32, freqs)[None, :]).reshape(-1)
    phases = angles(ids)
    cosine = 0.25 * jnp.cos(phases)
    sine = 0.25 * jnp.sin(phases)
    index = window_index.reshape(1, points)

    took = gave = [((0, freqs, False),)] * CHUNKS
    if freqs > 2 and tiles > GROUP:
        took = [((0, freqs - 1, False), (freqs - 1, 1, True))] * CHUNKS
        took = [((0, 1, True), (1, freqs - 2, False), (freqs - 1, 1, True))] + took[1:]
        gave = gave[:-1] + [((0, 1, True), (1, freqs - 2, False), (freqs - 1, 1, True))]

    def runs(pieces):
        return tuple(piece[:2] for piece in pieces)

    sent = []
    token = None
    groups = tiles // GROUP
    for h in range(CHUNKS):
        jobs = [(n, 0, groups) for n in range(len(took[h]))]
        if h == 0 and took[h][0][2]:
            near = [(0, base, 1) for base in reversed(range(groups))]
            jobs[1:2] = [jobs[1]] + near[groups - groups // 2 :]
            jobs[:1] = near[: groups - groups // 2]
        made = [[] for _ in took[h]]
        for n, base, some in jobs:
            *piece, split = took[h][n]
            part = project(
                pos, col_factors, wavefield, piece, h, width, tiles, split, base, some, token
            )
            token = part[0] if split else part
            made[n] = [*part, *made[n]] if split else part
        sent.append([trade(made[n], tiles, took[h][n][2]) for n in range(len(took[h]))])
    back = []
    for h in range(CHUNKS):
        parts = []
        for n, (*piece, split) in enumerate(took[h]):
            made = expand(pos, row_factors, piece, sent[h][n], shares, token)
            token = made[0]
            parts.append([send(part, "freq", shares, m) for m, part in enumerate(made)])
        parts = window(cosine, sine, index, parts, runs(took[h]), runs(gave[h]), h)
        parts = [
            [send(part, "freq", shares, m) for m, part in enumerate(group)] for group in parts
        ]
        back.append([])
        token = None
        for n, (*piece, split) in enumerate(gave[h]):
            if n == 2:
                token = back[h - 1][0][0]
            made = contract(pos, row_factors, piece, parts[n], tiles, split, token)
            token = made[0] if split else made
            back[h].append(trade(made, tiles, split))
    result = None
    for h in range(CHUNKS):
        for n, (*piece, split) in enumerate(gave[h]):
            if n == 2:
                slow = tiles // GROUP // 2
                most = tuple(high for high in range(tiles // GROUP) if high != slow)
                part = None
                for highs in (most, (slow,)):
                    group = [back[h][n][high * GROUP + seat] for high in highs for seat in range(GROUP)]
                    ends = part is not None
                    part = finish(
                        pos, col_factors, piece, group, highs, h, points, part,
                        result if ends else None, None if ends else result,
                    )
                result = part
                continue
            result = spread(pos, col_factors, piece, back[h][n], h, points, result, token)
            token = None
    return result


def solution(mesh):
    spec = P("freq", None, "tile", None)
    body = functools.partial(local, mesh.shape["tile"], mesh.shape["freq"])
    return jax.shard_map(
        body, mesh=mesh, in_specs=(spec, spec, spec, P()), out_specs=spec, check_vma=False
    )
```

```python
import functools
import math

import jax
import jax.numpy as jnp
from jax import lax
from jax.experimental import pallas as pl
from jax.experimental.pallas import tpu as pltpu
from jax.sharding import PartitionSpec as P


TS = 512
RANK = 32
NT = 16
CHUNKS = 2
GROUP = 4
VMEM_BYTES = 67043328


def angles(freq_ids):
    times = lax.broadcasted_iota(jnp.int32, (NT, freq_ids.shape[0]), 0)
    return math.pi / NT * ((2 * freq_ids[None, :] + 1) * times).astype(jnp.float32)


def call(kernel, grid, prefetch, in_specs, out_specs, out_shape, scratch, flops, nbytes, after, **kw):
    count = prefetch + len(in_specs)
    inner = kernel
    if after is not None:
        in_specs = in_specs + [pl.BlockSpec(memory_space=pl.ANY)]

        def inner(*refs):
            kernel(*refs[:count], *refs[count + 1 :])

    made = pl.pallas_call(
        inner,
        grid_spec=pltpu.PrefetchScalarGridSpec(
            num_scalar_prefetch=prefetch,
            grid=grid,
            in_specs=in_specs,
            out_specs=out_specs,
            scratch_shapes=scratch,
        ),
        out_shape=out_shape,
        cost_estimate=pl.CostEstimate(flops=flops, bytes_accessed=nbytes, transcendentals=0),
        compiler_params=pltpu.CompilerParams(vmem_limit_bytes=VMEM_BYTES),
        **kw,
    )
    return made if after is None else lambda *args: made(*args, after)


def dot(left, right):
    return jnp.dot(left, right, preferred_element_type=jnp.float32)


def turned(left, right):
    return lax.dot_general(left, right, (((0,), (0,)), ((), ())), preferred_element_type=jnp.float32)


def project_kernel(dims, pos, v_ref, w_ref, *refs):
    size, groups, col_local, row_local, width, split = dims
    span = row_local * RANK
    outs = refs[: groups * size if split else 1]
    wave = refs[len(outs)]

    @pl.when(pl.program_id(1) == 0)
    def _():
        wave[:width] = w_ref[0, 0].T
        wave[width:] = w_ref[0, 1].T

    for c in range(col_local):
        rows = slice(c * TS, (c + 1) * TS)
        to = slice(c * RANK, (c + 1) * RANK)
        with_real = dot(wave[:, rows], v_ref[0, 0, rows])
        with_imag = dot(wave[:, rows], v_ref[0, 1, rows])
        real = with_real[:width] + with_imag[width:]
        imag = with_real[width:] - with_imag[:width]
        both = jnp.concatenate([real, imag], 0).astype(jnp.bfloat16).T
        if not split:
            for d in range(size):
                for i in range(row_local):
                    start = d * span + i * RANK
                    outs[0][d, 0, i, to] = both[start : start + RANK]
            continue
        stage = refs[-1]
        stage[...] = both
        for high in range(groups):

            @pl.when(pl.program_id(1) == high)
            def _():
                for low in range(size):
                    base = ((pos[0] % size) ^ low) * span
                    for i in range(row_local):
                        start = pl.multiple_of(base + i * RANK, RANK)
                        outs[high * size + low][0, i, to] = stage[pl.ds(start, RANK)]


def project(pos, col_factors, wavefield, piece, chunk, width, tiles, split, size, base, groups, after):
    first, freqs = piece
    _, _, src_rows, cols = col_factors.shape
    col_local = src_rows // TS
    row_local = cols // RANK // tiles
    lanes = size * row_local * RANK
    shape = (freqs, row_local, col_local * RANK, 2 * width)
    if split:
        out_specs = [pl.BlockSpec((1,) + shape[1:], lambda f, g, s: (f, 0, 0, 0))] * (groups * size)
        out_shape = [jax.ShapeDtypeStruct(shape, jnp.bfloat16)] * (groups * size)
    else:
        out_specs = pl.BlockSpec((size, 1) + shape[1:], lambda f, g, s: (g, f, 0, 0, 0))
        out_shape = jax.ShapeDtypeStruct((tiles,) + shape, jnp.bfloat16)
    return call(
        functools.partial(project_kernel, (size, groups, col_local, row_local, width, split)),
        (freqs, groups),
        1,
        [
            pl.BlockSpec(
                (1, 2, src_rows, lanes),
                lambda f, g, s: (first + f, 0, 0, (s[0] // size) ^ (base + g) if split else g),
            ),
            pl.BlockSpec((1, 2, src_rows, width), lambda f, g, s: (first + f, 0, 0, chunk)),
        ],
        out_specs,
        out_shape,
        [pltpu.VMEM((2 * width, src_rows), jnp.bfloat16)]
        + [pltpu.VMEM((lanes, 2 * width), jnp.bfloat16)] * split,
        8 * freqs * src_rows * groups * lanes * width,
        freqs * 4 * src_rows * (groups * lanes + 2 * width),
        after,
    )(pos, col_factors, wavefield)


def gather(pos, got, step, stage):
    if stage is None:
        return got[0][:, 0, 0].reshape(-1, got[0].shape[-1])
    for m, ref in enumerate(got):
        stage[pl.ds(pl.multiple_of((pos[0] ^ m) * step, step), step)] = ref[0, 0]
    return stage[...]


def expand_kernel(dims, pos, u_ref, *refs):
    count, shares, step, width = dims
    got, outs, stage = refs[:count], refs[count : count + shares], refs[count + shares]
    coeffs = gather(pos, got, step, refs[-1] if count > 1 else None)
    with_real = dot(u_ref[0, 0], coeffs)
    with_imag = dot(u_ref[0, 1], coeffs)
    stage[:, :width] = (with_real[:, :width] - with_imag[:, width:]).astype(jnp.bfloat16)
    stage[:, width:] = (with_real[:, width:] + with_imag[:, :width]).astype(jnp.bfloat16)
    share = TS // shares
    for g in range(shares):
        rows = pl.ds(pl.multiple_of((pos[1] ^ g) * share, share), share)
        outs[g][0, 0] = stage[rows]


def gather_specs(got, index):
    step, both = got[0].shape[-2:]
    if len(got) == 1:
        return [pl.BlockSpec((got[0].shape[0], 1, 1, step, both), lambda *n: (0,) + index(*n))], []
    stage = pltpu.VMEM((len(got) * step, both), got[0].dtype)
    return [pl.BlockSpec((1, 1, step, both), index)] * len(got), [stage]


def expand(pos, row_factors, piece, got, shares, after):
    first, freqs = piece
    _, _, rec_rows, cols = row_factors.shape
    row_local = rec_rows // TS
    step, both = got[0].shape[-2:]
    shape = (freqs, row_local, TS // shares, both)
    specs, scratch = gather_specs(got, lambda f, i, s: (f, i, 0, 0))
    return call(
        functools.partial(expand_kernel, (len(got), shares, step, both // 2)),
        (freqs, row_local),
        1,
        [pl.BlockSpec((1, 2, TS, cols), lambda f, i, s: (first + f, 0, i, 0))] + specs,
        [pl.BlockSpec((1, 1, TS // shares, both), lambda f, i, s: (f, i, 0, 0))] * shares,
        [jax.ShapeDtypeStruct(shape, jnp.bfloat16)] * shares,
        [pltpu.VMEM((TS, both), jnp.bfloat16)] + scratch,
        4 * freqs * rec_rows * cols * both,
        freqs * 2 * (rec_rows * (2 * cols + both) + row_local * cols * both),
        after,
    )(pos, row_factors, *got)


def window_kernel(dims, cosine, sine, index_ref, *refs):
    shares, took, gave, rows, slab, width = dims
    ins, outs = refs[: shares * len(took)], refs[shares * len(took) :]
    half = NT // 2
    masks = [t < index_ref[...] for t in range(NT)]

    def planes(arrays, pieces):
        return [
            (arrays[p * shares + g], f)
            for g in range(shares)
            for p, (_, freqs) in enumerate(pieces)
            for f in range(freqs)
        ]

    def body(n, carry):
        at = pl.ds(pl.multiple_of(n * slab, slab), slab)
        real = [ref[f, 0, at, :width].astype(jnp.float32) for ref, f in planes(ins, took)]
        imag = [ref[f, 0, at, width:].astype(jnp.float32) for ref, f in planes(ins, took)]
        count = len(real)
        even = [sum(cosine[t, k] * real[k] for k in range(count)) for t in range(half)]
        odd = [None] + [sum(sine[t, k] * imag[k] for k in range(count)) for t in range(1, half + 1)]
        zero = jnp.zeros_like(real[0])

        def keep(t, value):
            return jnp.where(masks[t], value, zero)

        diff = [keep(0, even[0])]
        total = [None]
        for t in range(1, half):
            one = keep(t, even[t] - odd[t])
            other = keep(NT - t, -even[t] - odd[t])
            diff.append(one - other)
            total.append(one + other)
        total.append(keep(half, -odd[half]))
        for k, (ref, f) in enumerate(planes(outs, gave)):
            out = sum(cosine[t, k] * diff[t] for t in range(half))
            ref[f, 0, at, :width] = out.astype(jnp.bfloat16)
            out = -sum(sine[t, k] * total[t] for t in range(1, half + 1))
            ref[f, 0, at, width:] = out.astype(jnp.bfloat16)
        return carry

    lax.fori_loop(0, rows // slab, body, 0)


def window(cosine, sine, index, parts, took, gave, chunk):
    shares = len(parts[0])
    _, row_local, rows, both = parts[0][0].shape

    def spec(freqs):
        return pl.BlockSpec((freqs, 1, rows, both), lambda i, c, s: (0, i, 0, 0))

    size = sum(part.size for group in parts for part in group)
    made = call(
        functools.partial(window_kernel, (shares, took, gave, rows, 16, both // 2)),
        (row_local,),
        2,
        [pl.BlockSpec((1, both // 2), lambda i, c, s: (0, chunk))]
        + [spec(freqs) for _, freqs in took for _ in range(shares)],
        [spec(freqs) for _, freqs in gave for _ in range(shares)],
        [
            jax.ShapeDtypeStruct((freqs, row_local, rows, both), jnp.bfloat16)
            for _, freqs in gave
            for _ in range(shares)
        ],
        [],
        2 * NT * size,
        4 * size,
        None,
    )(cosine, sine, index, *[part for group in parts for part in group])
    return [made[p * shares : (p + 1) * shares] for p in range(len(gave))]


def contract_kernel(dims, pos, u_ref, *refs):
    tiles, shares, col_local, width, split = dims
    ins, outs = refs[:shares], refs[shares : shares + (tiles if split else 1)]
    stage = refs[shares + len(outs)]
    share = TS // shares
    for g in range(shares):
        stage[pl.ds(pl.multiple_of((pos[1] ^ g) * share, share), share)] = ins[g][0, 0]
    with_real = turned(stage[...], u_ref[0, 0])
    with_imag = turned(stage[...], u_ref[0, 1])
    real = with_real[:width] + with_imag[width:]
    imag = with_real[width:] - with_imag[:width]
    both = jnp.concatenate([real, imag], 0).astype(jnp.bfloat16).T
    if not split:
        outs[0][:, 0] = both.reshape(tiles, col_local, RANK, 2 * width)
        return
    rows = refs[-1]
    rows[...] = both
    for m in range(tiles):
        for c in range(col_local):
            start = ((pos[0] ^ m) * col_local + c) * RANK
            outs[m][0, c] = rows[pl.ds(pl.multiple_of(start, RANK), RANK)]


def contract(pos, row_factors, piece, parts, tiles, split, after):
    first, freqs = piece
    _, _, rec_rows, cols = row_factors.shape
    row_local = rec_rows // TS
    shares = len(parts)
    share, both = parts[0].shape[2:]
    col_local = cols // RANK // tiles
    shape = (freqs, col_local, row_local * RANK, both)
    if split:
        out_specs = [pl.BlockSpec((1, col_local, RANK, both), lambda f, i, s: (f, 0, i, 0))] * tiles
        out_shape = [jax.ShapeDtypeStruct(shape, jnp.bfloat16)] * tiles
    else:
        out_specs = pl.BlockSpec((tiles, 1, col_local, RANK, both), lambda f, i, s: (0, f, 0, i, 0))
        out_shape = jax.ShapeDtypeStruct((tiles,) + shape, jnp.bfloat16)
    return call(
        functools.partial(contract_kernel, (tiles, shares, col_local, both // 2, split)),
        (freqs, row_local),
        1,
        [pl.BlockSpec((1, 2, TS, cols), lambda f, i, s: (first + f, 0, i, 0))]
        + [pl.BlockSpec((1, 1, share, both), lambda f, i, s: (f, i, 0, 0))] * shares,
        out_specs,
        out_shape,
        [pltpu.VMEM((TS, both), jnp.bfloat16)] + [pltpu.VMEM((cols, both), jnp.bfloat16)] * split,
        4 * freqs * rec_rows * cols * both,
        freqs * 2 * (rec_rows * (2 * cols + both) + row_local * cols * both),
        after,
    )(pos, row_factors, *parts)


def spread_kernel(dims, pos, v_ref, *refs):
    count, carried, step, width = dims
    got, out = refs[:count], refs[count + carried]
    coeffs = gather(pos, got, step, refs[-1] if count > 1 else None)
    with_real = dot(v_ref[0, 0], coeffs)
    with_imag = dot(v_ref[0, 1], coeffs)
    out[0, 0] = with_real[:, :width] - with_imag[:, width:]
    out[0, 1] = with_real[:, width:] + with_imag[:, :width]


def spread(pos, col_factors, piece, got, chunk, points, before, after):
    first, freqs = piece
    total, _, src_rows, cols = col_factors.shape
    step, both = got[0].shape[-2:]
    carried = 0 if before is None else 1
    specs, scratch = gather_specs(got, lambda f, c, s: (f, c, 0, 0))
    return call(
        functools.partial(spread_kernel, (len(got), carried, step, both // 2)),
        (freqs, src_rows // TS),
        1,
        [pl.BlockSpec((1, 2, TS, cols), lambda f, c, s: (first + f, 0, c, 0))]
        + specs
        + [pl.BlockSpec(memory_space=pl.ANY)] * carried,
        pl.BlockSpec((1, 2, TS, both // 2), lambda f, c, s: (first + f, 0, c, chunk)),
        jax.ShapeDtypeStruct((total, 2, src_rows, points), jnp.float32),
        scratch,
        4 * freqs * src_rows * cols * both,
        freqs * 4 * (src_rows * (cols + both) + cols * both),
        after,
        input_output_aliases={2 + len(got): 0} if carried else {},
    )(pos, col_factors, *got, *([before] if carried else []))


def finish_kernel(dims, pos, *refs):
    groups, step, width, adds = dims
    held, got = refs[:groups], refs[groups : groups * (1 + GROUP)]
    out, stage = refs[-2:]
    with_real = with_imag = 0.0
    for n, v_ref in enumerate(held):
        for seat in range(GROUP):
            row = ((pos[0] % GROUP) ^ seat) * step
            stage[n, pl.ds(pl.multiple_of(row, step), step)] = got[n * GROUP + seat][0, 0]
        with_real = with_real + dot(v_ref[0, 0], stage[n])
        with_imag = with_imag + dot(v_ref[0, 1], stage[n])
    real = with_real[:, :width] - with_imag[:, width:]
    imag = with_real[:, width:] + with_imag[:, :width]
    if adds:
        part = refs[groups * (1 + GROUP)]
        real, imag = part[0, 0] + real, part[0, 1] + imag
    out[0, 0] = real
    out[0, 1] = imag


def finish(pos, col_factors, piece, got, highs, chunk, points, part, before, after):
    first, freqs = piece
    total, _, src_rows, _ = col_factors.shape
    step, both = got[0].shape[-2:]
    width, groups = both // 2, len(highs)
    own = pl.BlockSpec((1, 2, TS, width), lambda f, c, s: (f, 0, c, 0))
    last = before is not None
    adds = part is not None
    shape = (total, 2, src_rows, points) if last else (freqs, 2, src_rows, width)

    def held(high):
        return pl.BlockSpec(
            (1, 2, TS, GROUP * step), lambda f, c, s: (first + f, 0, c, (s[0] // GROUP) ^ high)
        )

    return call(
        functools.partial(finish_kernel, (groups, step, width, adds)),
        (freqs, src_rows // TS),
        1,
        [held(high) for high in highs]
        + [pl.BlockSpec((1, 1, step, both), lambda f, c, s: (f, c, 0, 0))] * len(got)
        + [own] * adds
        + [pl.BlockSpec(memory_space=pl.ANY)] * last,
        pl.BlockSpec((1, 2, TS, width), lambda f, c, s: (first + f, 0, c, chunk)) if last else own,
        jax.ShapeDtypeStruct(shape, jnp.float32),
        [pltpu.VMEM((groups, GROUP * step, both), got[0].dtype)],
        4 * freqs * src_rows * len(got) * step * both,
        freqs * 4 * (src_rows * (len(got) * step + both) + len(got) * step * both),
        after,
        input_output_aliases={1 + groups + len(got) + adds: 0} if last else {},
    )(pos, *[col_factors] * groups, *got, *([part] if adds else []), *([before] if last else []))


def send(array, axis, size, mask):
    if mask == 0:
        return array
    return lax.ppermute(array, axis, [(n, n ^ mask) for n in range(size)])


def trade(made, tiles, split):
    if not split:
        return [lax.all_to_all(made, "tile", 0, 0, tiled=True)]
    got = list(made)
    for m in reversed(range(tiles)):
        got[m] = send(made[m], "tile", tiles, m)
    return got


def local(tiles, shares, wavefield, row_factors, col_factors, window_index):
    freqs = wavefield.shape[0]
    points = wavefield.shape[3]
    width = points // CHUNKS
    share = lax.axis_index("freq")
    pos = jnp.stack([lax.axis_index("tile"), share]).astype(jnp.int32)
    owners = share ^ lax.iota(jnp.int32, shares)
    ids = (owners[:, None] * freqs + lax.iota(jnp.int32, freqs)[None, :]).reshape(-1)
    phases = angles(ids)
    cosine = 0.25 * jnp.cos(phases)
    sine = 0.25 * jnp.sin(phases)
    index = window_index.reshape(1, points)

    took = gave = [((0, freqs, False),)] * CHUNKS
    if freqs > 2 and tiles > GROUP:
        took = [((0, freqs - 1, False), (freqs - 1, 1, True))] * CHUNKS
        took = [((0, 1, True), (1, freqs - 2, False), (freqs - 1, 1, True))] + took[1:]
        gave = gave[:-1] + [((0, 1, True), (1, freqs - 2, False), (freqs - 1, 1, True))]

    def runs(pieces):
        return tuple(piece[:2] for piece in pieces)

    sent = []
    token = None
    groups = tiles // GROUP
    for h in range(CHUNKS):
        jobs = [(n, GROUP, 0, groups) for n in range(len(took[h]))]
        if h == 0 and took[h][0][2]:
            near = [(0, GROUP, base, 1) for base in reversed(range(groups))]
            jobs[1:2] = [jobs[1]] + near[groups - groups // 2 :]
            half = GROUP // 2
            jobs[:1] = [(0, half, 2 * groups - 1, 1), (0, half, 2 * groups - 2, 1)]
            jobs[2:2] = near[1 : groups - groups // 2]
        made = [[] for _ in took[h]]
        for n, size, base, some in jobs:
            *piece, split = took[h][n]
            part = project(
                pos, col_factors, wavefield, piece, h, width, tiles, split, size, base, some, token
            )
            token = part[0] if split else part
            made[n] = [*part, *made[n]] if split else part
        sent.append([trade(made[n], tiles, took[h][n][2]) for n in range(len(took[h]))])
    back = []
    for h in range(CHUNKS):
        parts = []
        for n, (*piece, split) in enumerate(took[h]):
            made = expand(pos, row_factors, piece, sent[h][n], shares, token)
            token = made[0]
            parts.append([send(part, "freq", shares, m) for m, part in enumerate(made)])
        parts = window(cosine, sine, index, parts, runs(took[h]), runs(gave[h]), h)
        parts = [
            [send(part, "freq", shares, m) for m, part in enumerate(group)] for group in parts
        ]
        back.append([])
        token = None
        for n, (*piece, split) in enumerate(gave[h]):
            if n == 2:
                token = back[h - 1][0][0]
            made = contract(pos, row_factors, piece, parts[n], tiles, split, token)
            token = made[0] if split else made
            back[h].append(trade(made, tiles, split))
    result = None
    for h in range(CHUNKS):
        for n, (*piece, split) in enumerate(gave[h]):
            if n == 2:
                slow = tiles // GROUP // 2
                most = tuple(high for high in range(tiles // GROUP) if high != slow)
                part = None
                for highs in (most, (slow,)):
                    group = [back[h][n][high * GROUP + seat] for high in highs for seat in range(GROUP)]
                    ends = part is not None
                    part = finish(
                        pos, col_factors, piece, group, highs, h, points, part,
                        result if ends else None, None if ends else result,
                    )
                result = part
                continue
            result = spread(pos, col_factors, piece, back[h][n], h, points, result, token)
            token = None
    return result


def solution(mesh):
    spec = P("freq", None, "tile", None)
    body = functools.partial(local, mesh.shape["tile"], mesh.shape["freq"])
    return jax.shard_map(
        body, mesh=mesh, in_specs=(spec, spec, spec, P()), out_specs=spec, check_vma=False
    )
```
